32 devices in a mesh: band: 2 (over y), member: 16 (over z, x, core).
Axes of the slice: x: 2, y: 2, z: 4, core: 2. Of those that a mesh axis runs over, the one named last changes fastest.
Arguments:
- ensemble: bfloat16 [128, 4, 64, 1024], P('member', None, 'band'), may hold values from -6 to 6
- variance: float32 [4, 64, 1024], P(None, 'band'), may hold values from 0.25 to 4
- obs_index: int32 [16, 8192], P('member', 'band'), may hold values from 0 to 131071
- obs_value: float32 [16, 8192], P('member', 'band'), may hold values from -8 to 8
- obs_error: float32 [16, 8192], P('member', 'band'), may hold values from 0.5 to 2
- root_ranks: int32 [2], replicated, may hold values from 0 to 15
Outputs:
- increment: float32 [4, 64, 1024], P(None, 'band')
The draws below stay inside these ranges and needn't reach their ends.
Inputs may be any that keep to these rules, and one draw needn't show every extreme that they name: `obs_index`: the position level * 32 * 1024 + row within the band * 1024 + longitude; columns b * 4096 to (b + 1) * 4096 - 1 belong to band b; positions may repeat.
All inputs are finite; a program needn't handle non-finite values.
Results may differ from the reference program's by a relative error of at most 0.0024.
Values may be sent and summed in bfloat16 or wider, within the bound.
No kernel may reach another device: no remote copies, remote signals or barrier semaphores. Data moves between devices by JAX's collectives and lax.ppermute only.
A program may use at most 64 MiB of HBM per device.

```python
import math
import jax
import jax.numpy as jnp
from jax import lax

LEV = 4
LAT_DEV = 32
LON = 1024
HALF = 8
MEM_DEV = 8
NOBS = 4096
ITERS = 2
MEMBERS = 128
NLAT = 64
BLOCKS = 16
BANDOBS = 8192
N_BAND = 2
N_MEMBER = 16


def place_ends(entries, stream_key, least, largest):
    extent = entries.shape
    spot = [jax.random.randint(jax.random.fold_in(stream_key, axis), (), 0, extent[axis]) for axis in range(len(extent))]
    entries = entries.at[tuple(spot)].set(least)
    longest = extent.index(max(extent))
    spot[longest] = (spot[longest] + 1) % extent[longest]
    return entries.at[tuple(spot)].set(largest)


def steps_of(rng, dims, shards, smallest, high):
    factor_of, own = 1.0, jax.random.fold_in(rng, 6)
    for position, shards_of in shards:
        draws = jnp.exp(jax.random.uniform(jax.random.fold_in(own, position), (shards_of,), jnp.float32, smallest / len(shards), high / len(shards)))
        factor_of = factor_of * jnp.repeat(draws, dims[position] // shards_of).reshape([-1 if axis == position else 1 for axis in range(len(dims))])
    return factor_of


def scatter_about(rng, extent, width, reach, cuts=(), kind=jnp.bfloat16):
    factor_of = steps_of(rng, extent, cuts, -0.22, 0.18) if cuts else 1.0
    array = jax.random.normal(rng, extent, jnp.float32) * width * factor_of
    return jnp.minimum(jnp.maximum(array, -reach), reach).astype(kind)


def setup_inputs(seed: int = 0) -> dict:
    streams_of = jax.random.split(jax.random.key(seed), 7)
    ensemble = scatter_about(streams_of[0], (MEMBERS, LEV, NLAT, LON), 1.0, 6.0, ((0, 16), (2, 2)))
    variance = jnp.clip(jnp.exp(math.log(4.0) - 2.7725887 * jax.random.uniform(streams_of[1], (LEV, NLAT, LON), jnp.float32) ** steps_of(streams_of[1], (LEV, NLAT, LON), ((1, 2),), -0.2, 0.2)), 0.25, 4.0)
    obs_index = place_ends(jax.random.randint(streams_of[2], (BLOCKS, BANDOBS), 0, LEV * LAT_DEV * LON), jax.random.fold_in(streams_of[2], 1), 0, (LEV * LAT_DEV * LON) - 1).astype(jnp.int32)
    obs_value = scatter_about(streams_of[3], (BLOCKS, BANDOBS), 2.0, 8.0, ((0, 16), (1, 2)), jnp.float32)
    obs_error = jnp.clip(jnp.exp(math.log(2.0) - 1.3862944 * jax.random.uniform(streams_of[4], (BLOCKS, BANDOBS), jnp.float32) ** steps_of(streams_of[4], (BLOCKS, BANDOBS), ((0, 16), (1, 2)), -0.2, 0.2)), 0.5, 2.0)
    root_ranks = jax.random.randint(streams_of[5], (ITERS,), 0, N_MEMBER).astype(jnp.int32)
    return dict(ensemble=ensemble, variance=variance, obs_index=obs_index, obs_value=obs_value, obs_error=obs_error, root_ranks=root_ranks)


huber_edge = 1.5
ensemble_share = 0.75
static_share = 0.25

def tap_table(radius):
    offsets = jnp.arange(-radius, radius + 1).astype(jnp.float32)
    raw = jnp.exp(-0.5 * (offsets / (0.5 * radius)) ** 2)
    return (raw / jnp.sqrt(jnp.sum(raw * raw))).astype(jnp.bfloat16).astype(jnp.float32)

def along_lon(values, table):
    source = values.astype(jnp.float32)
    total = jnp.zeros(source.shape, jnp.float32)
    for shift in range(-HALF, HALF + 1):
        total = total + table[shift + HALF] * jnp.roll(source, shift, axis=-1)
    return total

def along_lat(values, table):
    source = values.astype(jnp.float32)
    padded = jnp.pad(source, ((0, 0), (0, 0), (HALF, HALF), (0, 0)))
    total = jnp.zeros(source.shape, jnp.float32)
    for shift in range(-HALF, HALF + 1):
        total = total + table[shift + HALF] * padded[:, :, HALF + shift:HALF + shift + NLAT, :]
    return total

def reference(ensemble, variance, obs_index, obs_value, obs_error, root_ranks):
    table = tap_table(HALF)
    field = jnp.zeros((LEV, NLAT, LON), jnp.float32)
    band_of = (jnp.arange(NOBS * N_BAND) // NOBS).astype(jnp.int32)
    blocks = ensemble.reshape(N_MEMBER, MEM_DEV, LEV, NLAT, LON)
    for iteration in range(ITERS):
        block = root_ranks[iteration]
        local = obs_index[block].astype(jnp.int32)
        level = local // (LAT_DEV * LON)
        row_pos = band_of * LAT_DEV + local // LON % LAT_DEV
        column = local % LON
        place = ((level * NLAT + row_pos) * LON + column).astype(jnp.int32)
        values = obs_value[block]
        errors = obs_error[block]
        departure = values - field.reshape(-1)[place]
        weight = huber_edge / jnp.maximum(jnp.abs(departure / errors), huber_edge)
        gradient = jnp.zeros((LEV * NLAT * LON,), jnp.float32).at[place].add(weight * departure / (errors * errors)).reshape(LEV, NLAT, LON)

        def one_block(total, members):
            wide = members.astype(jnp.float32)
            mixed = (wide * gradient[None]).astype(jnp.bfloat16)
            first = along_lon(mixed, table).astype(jnp.bfloat16)
            first = along_lat(first, table).astype(jnp.bfloat16)
            second = along_lon(first, table).astype(jnp.bfloat16)
            second = along_lat(second, table)
            return (total + lax.optimization_barrier(jnp.sum(wide * second, axis=0)), None)
        spread, _ = lax.scan(one_block, jnp.zeros((LEV, NLAT, LON), jnp.float32), blocks)
        direction = ensemble_share * spread / (MEMBERS - 1) + static_share * variance * gradient
        along = jnp.sum(gradient * direction)
        back = jnp.sum(field * gradient)
        reached = direction.reshape(-1)[place]
        curve = jnp.sum(weight * reached * reached / (errors * errors))
        field = field + (along - back) / (along + curve) * direction
    return field
```

```python
import functools

import jax
import jax.numpy as jnp
from jax import lax
from jax.experimental import pallas as pl
from jax.experimental.pallas import tpu as pltpu
from jax.sharding import PartitionSpec as P

HALF = 8
ITERS = 2
REACH = 2 * HALF

huber_edge = 1.5
ensemble_share = 0.75
static_share = 0.25

LANES = 256
F32 = jnp.float32
BF16 = jnp.bfloat16


def tap_matrix(distance, radius):
    offsets = jnp.arange(-radius, radius + 1).astype(F32)
    raw = jnp.exp(-0.5 * (offsets / (0.5 * radius)) ** 2)
    norm_value = jnp.sqrt(jnp.sum(raw * raw))
    scaled = distance.astype(F32) / (0.5 * radius)
    entry = jnp.exp(-0.5 * scaled**2) / norm_value
    return jnp.where(jnp.abs(distance) <= radius, entry, 0.0).astype(BF16)


def lon_tile(radius):
    source = jnp.arange(2 * LANES)[:, None] - LANES // 2
    target = jnp.arange(LANES)[None, :]
    return tap_matrix(source - target, radius)


def lat_block(out_level, out_row, in_level, in_row, rows_total, radius):
    distance = in_row[None, :] - out_row[:, None]
    entry = tap_matrix(distance, radius)
    inside = (out_row >= 0) & (out_row < rows_total)
    keep = (out_level[:, None] == in_level[None, :]) & inside[:, None]
    return jnp.where(keep, entry, 0).astype(BF16)


def split_bf16(x):
    hi = x.astype(BF16)
    lo = (x - hi.astype(F32)).astype(BF16)
    return hi, lo


def onehot(index, count):
    rows = lax.broadcasted_iota(jnp.int32, (count, index.shape[1]), 0)
    return jnp.where(rows == index, 1.0, 0.0).astype(BF16)


def scatter_kernel(lon, rows, sources, *refs):
    start_ref, own_idx, own_coef = refs[:3]
    ext = refs[3:3 + 2 * sources]
    own_out, ext_out, own_acc, ext_acc = refs[3 + 2 * sources:]
    blocks = lon // LANES
    chunks = own_idx.shape[0]
    row_bits = lon

    def add(idx, coef, seg, acc):
        lane = idx % LANES
        hi, lo = split_bf16(coef)
        spot = lax.broadcasted_iota(jnp.int32, (LANES, idx.shape[1]), 0) == lane
        side = jnp.concatenate(
            [
                jnp.where(spot, hi.astype(F32), 0.0).astype(BF16),
                jnp.where(spot, lo.astype(F32), 0.0).astype(BF16),
            ],
            axis=0,
        )
        hot = onehot(seg, acc.shape[0])
        acc[...] += lax.dot_general(
            hot, side, (((1,), (1,)), ((), ())), preferred_element_type=F32
        )

    own_acc[...] = jnp.zeros_like(own_acc)
    ext_acc[...] = jnp.zeros_like(ext_acc)
    own_rows = own_out.shape[0]
    ext_rows = ext_out.shape[0] // sources
    for c in range(chunks):
        idx = own_idx[c:c + 1, :].astype(jnp.int32)
        blk = (idx % lon) // LANES
        add(idx, own_coef[c:c + 1, :], blk * own_rows + idx // row_bits, own_acc)
        for s in range(sources):
            idx = ext[2 * s][c:c + 1, :].astype(jnp.int32)
            blk = (idx % lon) // LANES
            level = idx // (row_bits * rows)
            row = (idx // row_bits) % rows - start_ref[s]
            inside = (row >= 0) & (row < REACH)
            seg = blk * ext_rows + level * REACH + row
            seg = jnp.where(inside, seg, -1)
            add(idx, ext[2 * s + 1][c:c + 1, :], seg, ext_acc.at[s])
    for b in range(blocks):
        lanes = slice(b * LANES, (b + 1) * LANES)
        part = own_acc[b * own_rows:(b + 1) * own_rows, :]
        own_out[:, lanes] = part[:, :LANES] + part[:, LANES:]
        for s in range(sources):
            part = ext_acc[s, b * ext_rows:(b + 1) * ext_rows, :]
            ext_out[s * ext_rows:(s + 1) * ext_rows, lanes] = part[:, :LANES] + part[:, LANES:]


def scatter_obs(levels, rows, lon, starts, own, ext):
    sources = len(ext)
    blocks = lon // LANES
    own_rows, ext_rows = levels * rows, levels * REACH
    vm = pl.BlockSpec(memory_space=pltpu.VMEM)
    args = [starts, *own]
    for pair in ext:
        args += list(pair)
    return pl.pallas_call(
        functools.partial(scatter_kernel, lon, rows, sources),
        out_shape=(
            jax.ShapeDtypeStruct((own_rows, lon), F32),
            jax.ShapeDtypeStruct((sources * ext_rows, lon), F32),
        ),
        in_specs=[pl.BlockSpec(memory_space=pltpu.SMEM)] + [vm] * (len(args) - 1),
        out_specs=(vm, vm),
        scratch_shapes=[
            pltpu.VMEM((blocks * own_rows, 2 * LANES), F32),
            pltpu.VMEM((sources, blocks * ext_rows, 2 * LANES), F32),
        ],
        name="scatter_obs",
    )(*args)


def lon_pass(x, tile):
    lon = x.shape[1]
    half = LANES // 2
    parts = []
    for j in range(lon // LANES):
        lo, hi = j * LANES - half, (j + 1) * LANES + half
        if lo < 0:
            window = jnp.concatenate([x[:, lon + lo:], x[:, :hi]], axis=1)
        elif hi > lon:
            window = jnp.concatenate([x[:, lo:], x[:, :hi - lon]], axis=1)
        else:
            window = x[:, lo:hi]
        parts.append(jnp.dot(window, tile, preferred_element_type=F32).astype(BF16))
    return jnp.concatenate(parts, axis=1)


def filter_kernel(share, own_ref, ext_ref, grad_ref, gext_ref, var_ref, static_ref,
                  tile_ref, lat1_ref, lat2_ref, out_ref):
    step = pl.program_id(0)
    own = own_ref[0].astype(F32)
    ext = ext_ref[0].astype(F32)
    mixed = jnp.concatenate(
        [(own * grad_ref[...]).astype(BF16), (ext * gext_ref[...]).astype(BF16)], axis=0
    )
    tile = tile_ref[...]
    first = lon_pass(mixed, tile)
    first = jnp.dot(lat1_ref[...], first, preferred_element_type=F32).astype(BF16)
    second = lon_pass(first, tile)
    second = jnp.dot(lat2_ref[...], second, preferred_element_type=F32)
    product = own * second * share

    @pl.when(step == 0)
    def _():
        out_ref[...] = static_ref[0] * var_ref[...] * grad_ref[...] + product

    @pl.when(step > 0)
    def _():
        out_ref[...] += product


def filter_members(share, own, ext, grad, gext, variance, static, tile, lat1, lat2):
    members, rows, lon = own.shape
    whole = lambda a: pl.BlockSpec(a.shape, lambda i: (0,) * a.ndim)
    return pl.pallas_call(
        functools.partial(filter_kernel, share),
        grid=(members,),
        out_shape=jax.ShapeDtypeStruct((rows, lon), F32),
        in_specs=[
            pl.BlockSpec((1,) + own.shape[1:], lambda i: (i, 0, 0)),
            pl.BlockSpec((1,) + ext.shape[1:], lambda i: (i, 0, 0)),
            whole(grad), whole(gext), whole(variance),
            pl.BlockSpec(memory_space=pltpu.SMEM),
            whole(tile), whole(lat1), whole(lat2),
        ],
        out_specs=pl.BlockSpec((rows, lon), lambda i: (0, 0)),
        name="filter_members",
    )(own, ext, grad, gext, variance, static, tile, lat1, lat2)


def gather_kernel(lon, precise, field_ref, *refs):
    count = len(precise)
    idx_refs, out_ref, table = refs[:count], refs[count], refs[count + 1]
    rows = field_ref.shape[0]
    blocks = lon // LANES
    for b in range(blocks):
        part = field_ref[:, b * LANES:(b + 1) * LANES]
        turned = jnp.transpose(part)
        hi, lo = split_bf16(turned)
        table[:LANES, b * rows:(b + 1) * rows] = hi
        table[LANES:, b * rows:(b + 1) * rows] = lo
    chunks = idx_refs[0].shape[0]
    for n, (idx_ref, exact) in enumerate(zip(idx_refs, precise)):
        source = table[...] if exact else table[:LANES, :]
        for c in range(chunks):
            idx = idx_ref[c:c + 1, :].astype(jnp.int32)
            blk = (idx % lon) // LANES
            hot = onehot(blk * rows + idx // lon, blocks * rows)
            found = jnp.dot(source, hot, preferred_element_type=F32)
            if exact:
                found = found[:LANES] + found[LANES:]
            spot = lax.broadcasted_iota(jnp.int32, found.shape, 0) == idx % LANES
            value = jnp.sum(jnp.where(spot, found, 0.0), axis=0, keepdims=True)
            out_ref[n * chunks + c:n * chunks + c + 1, :] = value


def gather_places(field, idx_list, precise):
    rows, lon = field.shape
    chunks = idx_list[0].shape[0]
    vm = pl.BlockSpec(memory_space=pltpu.VMEM)
    return pl.pallas_call(
        functools.partial(gather_kernel, lon, tuple(precise)),
        out_shape=jax.ShapeDtypeStruct((len(idx_list) * chunks, lon), F32),
        in_specs=[vm] * (1 + len(idx_list)),
        out_specs=vm,
        scratch_shapes=[pltpu.VMEM((2 * LANES, (lon // LANES) * rows), BF16)],
        name="gather_places",
    )(field, *idx_list)


def partner(count, bit):
    return [(j, j ^ bit) for j in range(count)]


def member_bits(count):
    bits, d = [], 1
    while d < count:
        bits.append(d)
        d *= 2
    assert d == count
    return bits


def sum_members(x, count):
    for bit in member_bits(count):
        x = x + lax.ppermute(x, "member", partner(count, bit))
    return x


def reduce_with_tail(x, tail, count, position):
    rows = x.shape[0]
    for bit in member_bits(count):
        half = rows // 2
        upper = (position // bit) % 2 == 1
        low, high = x[:half], x[half:]
        message = jnp.concatenate([jnp.where(upper, low, high), tail], axis=0)
        message = lax.ppermute(message, "member", partner(count, bit))
        x = jnp.where(upper, high, low) + message[:half]
        tail = tail + message[half:]
        rows = half
    return x, tail


def gather_rows(x, count, position):
    for bit in reversed(member_bits(count)):
        other = lax.ppermute(x, "member", partner(count, bit))
        upper = (position // bit) % 2 == 1
        x = jnp.concatenate([jnp.where(upper, other, x), jnp.where(upper, x, other)], axis=0)
    return x


def from_bands(x, count):
    if count == 2:
        return [lax.ppermute(x, "band", [(0, 1), (1, 0)])]
    up = [(i, i + 1) for i in range(count - 1)]
    down = [(j, i) for i, j in up]
    return [lax.ppermute(x, "band", up), lax.ppermute(x, "band", down)]


def band_halo(ens, count, position):
    rows = ens.shape[2]
    first, last = ens[:, :, :REACH], ens[:, :, rows - REACH:]
    if count == 2:
        edge = jnp.where(position == 0, last, first)
        return [lax.ppermute(edge, "band", [(0, 1), (1, 0)])]
    up = [(i, i + 1) for i in range(count - 1)]
    down = [(j, i) for i, j in up]
    return [lax.ppermute(last, "band", up), lax.ppermute(first, "band", down)]


def local(ensemble, variance, obs_index, obs_value, obs_error, root_ranks):
    members_here, levels, lat_rows, lon = ensemble.shape
    n_member, n_band = lax.axis_size("member"), lax.axis_size("band")
    member_pos, band_pos = lax.axis_index("member"), lax.axis_index("band")
    members = members_here * n_member
    total_rows = lat_rows * n_band
    shape = (obs_index.shape[1] // lon, lon)
    chunks = shape[0]

    if n_band == 2:
        starts = jnp.where(band_pos == 0, 0, lat_rows - REACH).reshape(1)
        near = [jnp.where(band_pos == 0, lat_rows, lat_rows - REACH)]
        near_inner = [jnp.where(band_pos == 0, lat_rows, lat_rows - HALF)]
    else:
        starts = jnp.array([lat_rows - REACH, 0])
        base = band_pos * lat_rows
        near = [base - REACH, base + lat_rows]
        near_inner = [base - HALF, base + lat_rows]
    starts = starts.astype(jnp.int32)

    level_of = jnp.arange(levels)
    def row_list(start, width):
        level = jnp.repeat(level_of, width)
        row = jnp.tile(jnp.arange(width), levels) + start
        return level, row
    own_rows = row_list(band_pos * lat_rows, lat_rows)
    outer = [own_rows] + [row_list(s, REACH) for s in near]
    inner = [own_rows] + [row_list(s, HALF) for s in near_inner]
    join = lambda parts: tuple(jnp.concatenate(p) for p in zip(*parts))
    outer, inner = join(outer), join(inner)
    lat1 = lat_block(*inner, *outer, total_rows, HALF)
    lat2 = lat_block(*own_rows, *inner, total_rows, HALF)
    tile = lon_tile(HALF)

    index = obs_index[0].reshape(shape).astype(F32)
    values = obs_value[0].reshape(shape)
    errors = obs_error[0].reshape(shape)
    weight = huber_edge / jnp.maximum(jnp.abs(values / errors), huber_edge)
    share_0 = weight / (errors * errors)
    block_0 = jnp.concatenate([index, share_0 * values, share_0], axis=0)
    block_1 = jnp.concatenate([index, values, errors], axis=0)
    message = jnp.concatenate(
        [
            jnp.where(member_pos == root_ranks[0], block_0, 0.0),
            jnp.where(member_pos == root_ranks[1], block_1, 0.0),
        ],
        axis=0,
    )
    halo = band_halo(ensemble, n_band, band_pos)
    message = sum_members(message, n_member)
    pieces = lambda a: [a[k * chunks:(k + 1) * chunks] for k in range(6)]
    index_0, coef_0, share_0, index_1, value_1, error_1 = pieces(message)
    near_parts = [pieces(a) for a in from_bands(message, n_band)]

    own = ensemble.reshape(members_here, levels * lat_rows, lon)
    ext = jnp.concatenate([h.reshape(members_here, levels * REACH, lon) for h in halo], axis=1)
    variance = variance.reshape(levels * lat_rows, lon)
    static = jnp.where(member_pos == 0, static_share, 0.0).reshape(1).astype(F32)
    share = ensemble_share / (members - 1)

    def direction_part(own_obs, ext_obs):
        grad, gext = scatter_obs(levels, lat_rows, lon, starts, own_obs, ext_obs)
        return filter_members(share, own, ext, grad, gext, variance, static, tile, lat1, lat2)

    part = direction_part((index_0, coef_0), [(p[0], p[1]) for p in near_parts])
    reached = gather_places(part, [index_0, index_1], [True, True])
    slice_0, reached = reduce_with_tail(part, reached, n_member, member_pos)
    reached_0, reached_1 = reached[:chunks], reached[chunks:]
    along = jnp.sum(coef_0 * reached_0)
    curve = jnp.sum(share_0 * reached_0 * reached_0)

    def band_sum(pair, extra):
        sums = jnp.broadcast_to(pair[:, None], (2, lon))
        text = jnp.concatenate([sums] + extra, axis=0)
        if n_band == 2:
            other = from_bands(text, n_band)
            return pair + other[0][:2, 0], [o[2:] for o in other]
        other = from_bands(text, n_band) if extra else []
        return lax.psum(pair, "band"), [o[2:] for o in other]

    (along, curve), near_reached = band_sum(jnp.stack([along, curve]), [reached_1])
    scale_0 = along / (along + curve)

    def weigh(at_place, value, error):
        departure = value - at_place
        weight = huber_edge / jnp.maximum(jnp.abs(departure / error), huber_edge)
        share = weight / (error * error)
        return share * departure, share

    field_1 = scale_0 * reached_1
    coef_1, share_1 = weigh(field_1, value_1, error_1)
    ext_obs = [
        (p[3], weigh(scale_0 * r, p[4], jnp.where(p[5] > 0, p[5], 1.0))[0])
        for p, r in zip(near_parts, near_reached)
    ]
    part = direction_part((index_1, coef_1), ext_obs)
    reached = gather_places(part, [index_1], [True])
    slice_1, reached = reduce_with_tail(part, reached, n_member, member_pos)
    along = jnp.sum(coef_1 * (reached - field_1))
    curve_along = jnp.sum(coef_1 * reached) + jnp.sum(share_1 * reached * reached)
    (along, curve_along), _ = band_sum(jnp.stack([along, curve_along]), [])
    scale_1 = along / curve_along
    out = scale_0 * slice_0 + scale_1 * slice_1
    out = gather_rows(out, n_member, member_pos)
    return out.reshape(levels, lat_rows, lon)


def solution(mesh):
    in_specs = (
        P("member", None, "band", None),
        P(None, "band", None),
        P("member", "band"),
        P("member", "band"),
        P("member", "band"),
        P(),
    )
    out_specs = P(None, "band", None)
    return jax.shard_map(local, mesh=mesh, in_specs=in_specs, out_specs=out_specs, check_vma=False)
```

```python
import functools

import jax
import jax.numpy as jnp
from jax import lax
from jax.experimental import pallas as pl
from jax.experimental.pallas import tpu as pltpu
from jax.sharding import PartitionSpec as P

HALF = 8
ITERS = 2
REACH = 2 * HALF

huber_edge = 1.5
ensemble_share = 0.75
static_share = 0.25

LANES = 256
F32 = jnp.float32
BF16 = jnp.bfloat16


def tap_matrix(distance, radius):
    offsets = jnp.arange(-radius, radius + 1).astype(F32)
    raw = jnp.exp(-0.5 * (offsets / (0.5 * radius)) ** 2)
    norm_value = jnp.sqrt(jnp.sum(raw * raw))
    scaled = distance.astype(F32) / (0.5 * radius)
    entry = jnp.exp(-0.5 * scaled**2) / norm_value
    return jnp.where(jnp.abs(distance) <= radius, entry, 0.0).astype(BF16)


def lon_tile(radius):
    source = jnp.arange(2 * LANES)[:, None] - LANES // 2
    target = jnp.arange(LANES)[None, :]
    return tap_matrix(source - target, radius)


def lat_block(out_level, out_row, in_level, in_row, rows_total, radius):
    distance = in_row[None, :] - out_row[:, None]
    entry = tap_matrix(distance, radius)
    inside = (out_row >= 0) & (out_row < rows_total)
    keep = (out_level[:, None] == in_level[None, :]) & inside[:, None]
    return jnp.where(keep, entry, 0).astype(BF16)


def split_bf16(x):
    hi = x.astype(BF16)
    lo = (x - hi.astype(F32)).astype(BF16)
    return hi, lo


def onehot(index, count):
    rows = lax.broadcasted_iota(jnp.int32, (count, index.shape[1]), 0)
    return jnp.where(rows == index, 1.0, 0.0).astype(BF16)


def vmem():
    return pl.BlockSpec(memory_space=pltpu.VMEM)


def smem():
    return pl.BlockSpec(memory_space=pltpu.SMEM)


def weigh(at_place, value, error):
    departure = value - at_place
    weight = huber_edge / jnp.maximum(jnp.abs(departure / error), huber_edge)
    share = weight / (error * error)
    return share * departure, share


def prepare_kernel(roots, idx_ref, value_ref, error_ref, out_ref):
    chunks, lon = out_ref.shape[0] // 6, out_ref.shape[1]
    position = lax.axis_index("member")
    first, second = position == roots[0], position == roots[1]
    for c in range(chunks):
        lanes = slice(c * lon, (c + 1) * lon)
        idx = idx_ref[:, lanes].astype(F32)
        value, error = value_ref[:, lanes], error_ref[:, lanes]
        coef, share = weigh(0.0, value, error)
        for k, x in enumerate((idx, coef, share)):
            out_ref[k * chunks + c:k * chunks + c + 1, :] = jnp.where(first, x, 0.0)
        for k, x in enumerate((idx, value, error)):
            k += 3
            out_ref[k * chunks + c:k * chunks + c + 1, :] = jnp.where(second, x, 0.0)


def prepare(roots, index, value, error, lon):
    return pl.pallas_call(
        prepare_kernel,
        out_shape=jax.ShapeDtypeStruct((6 * (index.shape[1] // lon), lon), F32),
        in_specs=[smem(), vmem(), vmem(), vmem()],
        out_specs=vmem(),
        name="prepare",
    )(roots, index, value, error)


def add_onehot(idx, coef, seg, acc):
    lane = idx % LANES
    hi, lo = split_bf16(coef)
    spot = lax.broadcasted_iota(jnp.int32, (LANES, idx.shape[1]), 0) == lane
    side = jnp.concatenate(
        [
            jnp.where(spot, hi.astype(F32), 0.0).astype(BF16),
            jnp.where(spot, lo.astype(F32), 0.0).astype(BF16),
        ],
        axis=0,
    )
    hot = onehot(seg, acc.shape[0])
    acc[...] += lax.dot_general(
        hot, side, (((1,), (1,)), ((), ())), preferred_element_type=F32
    )


def total_of(totals, row):
    value = totals[0][row:row + 1, :1]
    for t in totals[1:]:
        value = value + t[row:row + 1, :1]
    return value


def scale_of(totals, chunks):
    along = total_of(totals, chunks)
    return along / (along + total_of(totals, chunks + 1))


def coefficients(second, message, chunks, text, totals, c):
    row = lambda ref, k: ref[k * chunks + c:k * chunks + c + 1, :]
    if not second:
        return row(message, 0), row(message, 1)
    at_place = scale_of(totals, chunks) * row(text, 0)
    error = row(message, 5)
    coef, _ = weigh(at_place, row(message, 4), jnp.where(error > 0, error, 1.0))
    return row(message, 3), coef


def scatter_kernel(second, rows, lon, near, *refs):
    refs = list(refs)
    start_ref = refs.pop(0) if near is not None else None
    out_ref, acc = refs[-2:]
    message = refs[0]
    text, totals = (refs[1], refs[2:-2]) if second else (None, None)
    chunks = message.shape[0] // 6
    width = out_ref.shape[0]
    acc[...] = jnp.zeros_like(acc)
    for c in range(chunks):
        place, coef = coefficients(second, message, chunks, text, totals, c)
        idx = place.astype(jnp.int32)
        blk = (idx % lon) // LANES
        if near is None:
            seg = blk * width + idx // lon
        else:
            row = (idx // lon) % rows - start_ref[near]
            inside = (row >= 0) & (row < REACH)
            seg = blk * width + (idx // (lon * rows)) * REACH + row
            seg = jnp.where(inside, seg, -1)
        add_onehot(idx, coef, seg, acc)
    for b in range(lon // LANES):
        part = acc[b * width:(b + 1) * width, :]
        out_ref[:, b * LANES:(b + 1) * LANES] = part[:, :LANES] + part[:, LANES:]


def scatter_obs(levels, rows, lon, message, text, totals, near=None, starts=None):
    second = text is not None
    width = levels * (rows if near is None else REACH)
    args = [message] + ([text, *totals] if second else [])
    specs = [vmem()] * len(args)
    if near is not None:
        args, specs = [starts] + args, [smem()] + specs
    return pl.pallas_call(
        functools.partial(scatter_kernel, second, rows, lon, near),
        out_shape=jax.ShapeDtypeStruct((width, lon), F32),
        in_specs=specs,
        out_specs=vmem(),
        scratch_shapes=[pltpu.VMEM(((lon // LANES) * width, 2 * LANES), F32)],
        name="scatter_own" if near is None else "scatter_near",
    )(*args)


def lon_pass(x, tile):
    lon = x.shape[1]
    half = LANES // 2
    parts = []
    for j in range(lon // LANES):
        lo, hi = j * LANES - half, (j + 1) * LANES + half
        if lo < 0:
            window = jnp.concatenate([x[:, lon + lo:], x[:, :hi]], axis=1)
        elif hi > lon:
            window = jnp.concatenate([x[:, lo:], x[:, :hi - lon]], axis=1)
        else:
            window = x[:, lo:hi]
        parts.append(jnp.dot(window, tile, preferred_element_type=F32).astype(BF16))
    return jnp.concatenate(parts, axis=1)


def filter_kernel(share, own_ref, ext_ref, grad_ref, gext_ref, var_ref,
                  tile_ref, lat1_ref, lat2_ref, keep_ref, send_ref, acc_ref):
    step = pl.program_id(0)
    position = lax.axis_index("member")
    own = own_ref[0].astype(F32)
    ext = ext_ref[0].astype(F32)
    mixed = jnp.concatenate(
        [(own * grad_ref[...]).astype(BF16), (ext * gext_ref[...]).astype(BF16)], axis=0
    )
    tile = tile_ref[...]
    first = lon_pass(mixed, tile)
    first = jnp.dot(lat1_ref[...], first, preferred_element_type=F32).astype(BF16)
    second = lon_pass(first, tile)
    second = jnp.dot(lat2_ref[...], second, preferred_element_type=F32)
    product = own * second

    @pl.when(step == 0)
    def _():
        acc_ref[...] = product

    @pl.when(step > 0)
    def _():
        acc_ref[...] += product

    @pl.when(step == pl.num_programs(0) - 1)
    def _():
        half = keep_ref.shape[0]
        static = jnp.where(position == 0, static_share, 0.0)
        bit = position % 2
        for ref, start in ((keep_ref, bit * half), (send_ref, (1 - bit) * half)):
            rows = pl.ds(pl.multiple_of(start, half), half)
            ref[...] = share * acc_ref[rows, :] + static * var_ref[rows, :] * grad_ref[rows, :]


def filter_members(share, own, ext, grad, gext, variance, tile, lat1, lat2):
    members, rows, lon = own.shape
    whole = lambda a: pl.BlockSpec(a.shape, lambda i: (0,) * a.ndim)
    half = jax.ShapeDtypeStruct((rows // 2, lon), F32)
    return pl.pallas_call(
        functools.partial(filter_kernel, share),
        grid=(members,),
        out_shape=(half, half),
        in_specs=[
            pl.BlockSpec((1,) + own.shape[1:], lambda i: (i, 0, 0)),
            pl.BlockSpec((1,) + ext.shape[1:], lambda i: (i, 0, 0)),
            whole(grad), whole(gext), whole(variance),
            whole(tile), whole(lat1), whole(lat2),
        ],
        out_specs=(whole(half), whole(half)),
        scratch_shapes=[pltpu.VMEM((rows, lon), F32)],
        name="filter_members",
    )(own, ext, grad, gext, variance, tile, lat1, lat2)


def gather_kernel(which, keep_ref, got_ref, message, next_ref, send_ref):
    position = lax.axis_index("member")
    rows, lon = keep_ref.shape
    chunks = message.shape[0] // 6
    start = (position % 2) * rows
    field = keep_ref[...] + got_ref[...]
    low, high = field[:rows // 2], field[rows // 2:]
    upper = (position // 2) % 2 == 1
    next_ref[...] = jnp.where(upper, high, low)
    send_ref[:rows // 2, :] = jnp.where(upper, low, high)
    blocks = lon // LANES
    stacked = jnp.concatenate(
        [field[:, b * LANES:(b + 1) * LANES] for b in range(blocks)], axis=0
    )
    table = jnp.concatenate(split_bf16(jnp.transpose(stacked)), axis=0)
    for n, place in enumerate(which):
        for c in range(chunks):
            at = place * chunks + c
            idx = message[at:at + 1, :].astype(jnp.int32)
            blk = (idx % lon) // LANES
            row = idx // lon - start
            inside = (row >= 0) & (row < rows)
            hot = onehot(jnp.where(inside, blk * rows + row, -1), blocks * rows)
            found = jnp.dot(table, hot, preferred_element_type=F32)
            found = found[:LANES] + found[LANES:]
            spot = lax.broadcasted_iota(jnp.int32, found.shape, 0) == idx % LANES
            value = jnp.sum(jnp.where(spot, found, 0.0), axis=0, keepdims=True)
            at = rows // 2 + n * chunks + c
            send_ref[at:at + 1, :] = value


def gather_places(which, keep, got, message):
    rows, lon = keep.shape
    tail = len(which) * (message.shape[0] // 6)
    return pl.pallas_call(
        functools.partial(gather_kernel, which),
        out_shape=(
            jax.ShapeDtypeStruct((rows // 2, lon), F32),
            jax.ShapeDtypeStruct((rows // 2 + tail, lon), F32),
        ),
        in_specs=[vmem()] * 3,
        out_specs=(vmem(), vmem()),
        name="gather_places",
    )(keep, got, message)


def sums_kernel(second, *refs):
    tail, message, out_ref = refs[0], refs[1], refs[-1]
    chunks = message.shape[0] // 6
    lon = message.shape[1]
    part = lambda ref, k: ref[k * chunks:(k + 1) * chunks, :]
    total = lambda x: jnp.sum(jnp.sum(x, axis=0, keepdims=True), axis=1, keepdims=True)
    out_ref[...] = jnp.zeros_like(out_ref)
    reached = part(tail, 0)
    if second:
        text, totals = refs[2], refs[3:-1]
        at_place = scale_of(totals, chunks) * part(text, 0)
        coef, share = weigh(at_place, part(message, 4), part(message, 5))
        along = total(coef * (reached - at_place))
        curve = total(coef * at_place) + total(share * reached * reached)
    else:
        out_ref[:chunks, :] = part(tail, 1)
        along = total(part(message, 1) * reached)
        curve = total(part(message, 2) * reached * reached)
    out_ref[chunks:chunks + 1, :] = jnp.broadcast_to(along, (1, out_ref.shape[1]))
    out_ref[chunks + 1:chunks + 2, :] = jnp.broadcast_to(curve, (1, out_ref.shape[1]))


def sums(tail, message, text=None, totals=()):
    chunks, lon = message.shape[0] // 6, message.shape[1]
    second = text is not None
    args = [tail, message] + ([text, *totals] if second else [])
    rows = -(-(chunks + 2) // 8) * 8
    return pl.pallas_call(
        functools.partial(sums_kernel, second),
        out_shape=jax.ShapeDtypeStruct((rows, LANES // 2 if second else lon), F32),
        in_specs=[vmem()] * len(args),
        out_specs=vmem(),
        name="sums",
    )(*args)


def combine_kernel(chunks, count, *refs):
    pair, out_ref = refs[0], refs[-1]
    first, second = refs[1:1 + count], refs[1 + count:-1]
    scale_0 = scale_of(first, chunks)
    scale_1 = scale_of(second, chunks)
    out_ref[...] = scale_0 * pair[0] + scale_1 * pair[1]


def combine(pair, first, second, chunks):
    args = [pair, *first, *second]
    return pl.pallas_call(
        functools.partial(combine_kernel, chunks, len(first)),
        out_shape=jax.ShapeDtypeStruct(pair.shape[1:], F32),
        in_specs=[vmem()] * len(args),
        out_specs=vmem(),
        name="combine",
    )(*args)


def partner(count, bit):
    return [(j, j ^ bit) for j in range(count)]


def member_bits(count):
    bits, d = [], 1
    while d < count:
        bits.append(d)
        d *= 2
    assert d == count
    return bits


def swap(x, bit, count):
    return lax.ppermute(x, "member", partner(count, bit))


def reduce_with_tail(keep, send, bits, count, position):
    rows = keep.shape[0]
    for n, bit in enumerate(bits):
        got = swap(send, bit, count)
        x = keep + got[:rows]
        tail = send[rows:] + got[rows:]
        if n + 1 < len(bits):
            rows //= 2
            upper = (position // bits[n + 1]) % 2 == 1
            keep = jnp.where(upper, x[rows:], x[:rows])
            send = jnp.concatenate([jnp.where(upper, x[:rows], x[rows:]), tail], axis=0)
    return x, tail


def gather_rows(x, bit, count, position):
    other = swap(x, bit, count)
    upper = (position // bit) % 2 == 1
    axis = x.ndim - 2
    return jnp.concatenate([jnp.where(upper, other, x), jnp.where(upper, x, other)], axis=axis)


def from_bands(x, count):
    if count == 2:
        return [lax.ppermute(x, "band", [(0, 1), (1, 0)])]
    up = [(i, i + 1) for i in range(count - 1)]
    down = [(j, i) for i, j in up]
    return [lax.ppermute(x, "band", up), lax.ppermute(x, "band", down)]


def band_halo(ens, count, position):
    rows = ens.shape[2]
    first, last = ens[:, :, :REACH], ens[:, :, rows - REACH:]
    if count == 2:
        edge = jnp.where(position == 0, last, first)
        return [lax.ppermute(edge, "band", [(0, 1), (1, 0)])]
    up = [(i, i + 1) for i in range(count - 1)]
    down = [(j, i) for i, j in up]
    return [lax.ppermute(last, "band", up), lax.ppermute(first, "band", down)]


def local(ensemble, variance, obs_index, obs_value, obs_error, root_ranks):
    members_here, levels, lat_rows, lon = ensemble.shape
    n_member, n_band = lax.axis_size("member"), lax.axis_size("band")
    member_pos, band_pos = lax.axis_index("member"), lax.axis_index("band")
    members = members_here * n_member
    total_rows = lat_rows * n_band
    chunks = obs_index.shape[1] // lon
    bits = member_bits(n_member)

    if n_band == 2:
        starts = jnp.where(band_pos == 0, 0, lat_rows - REACH).reshape(1)
        near = [jnp.where(band_pos == 0, lat_rows, lat_rows - REACH)]
        near_inner = [jnp.where(band_pos == 0, lat_rows, lat_rows - HALF)]
    else:
        starts = jnp.array([lat_rows - REACH, 0])
        base = band_pos * lat_rows
        near = [base - REACH, base + lat_rows]
        near_inner = [base - HALF, base + lat_rows]
    starts = starts.astype(jnp.int32)

    level_of = jnp.arange(levels)
    def row_list(start, width):
        level = jnp.repeat(level_of, width)
        row = jnp.tile(jnp.arange(width), levels) + start
        return level, row
    own_rows = row_list(band_pos * lat_rows, lat_rows)
    outer = [own_rows] + [row_list(s, REACH) for s in near]
    inner = [own_rows] + [row_list(s, HALF) for s in near_inner]
    join = lambda parts: tuple(jnp.concatenate(p) for p in zip(*parts))
    outer, inner = join(outer), join(inner)
    lat1 = lat_block(*inner, *outer, total_rows, HALF)
    lat2 = lat_block(*own_rows, *inner, total_rows, HALF)
    tile = lon_tile(HALF)

    message = prepare(root_ranks, obs_index, obs_value, obs_error, lon)
    message = message + swap(message, bits[0], n_member)
    ensemble, message = lax.optimization_barrier((ensemble, message))
    halo = band_halo(ensemble, n_band, band_pos)
    for bit in bits[1:]:
        message = message + swap(message, bit, n_member)
    around = from_bands(message, n_band)

    own = ensemble.reshape(members_here, levels * lat_rows, lon)
    ext = jnp.concatenate([h.reshape(members_here, levels * REACH, lon) for h in halo], axis=1)
    variance = variance.reshape(levels * lat_rows, lon)
    share = ensemble_share / (members - 1)

    def direction_parts(text=None, totals=(), texts=()):
        scatter = functools.partial(scatter_obs, levels, lat_rows, lon)
        grad = scatter(message, text, totals)
        gext = [
            scatter(a, texts[s] if texts else None, totals, s, starts)
            for s, a in enumerate(around)
        ]
        gext = jnp.concatenate(gext, axis=0)
        keep, send = filter_members(share, own, ext, grad, gext, variance, tile, lat1, lat2)
        got = swap(send, bits[0], n_member)
        which = (3,) if texts else (0, 3)
        keep, send = gather_places(which, keep, got, message)
        piece, tail = reduce_with_tail(keep, send, bits[1:], n_member, member_pos)
        return piece, tail + swap(tail, bits[0], n_member)

    def band_totals(text):
        texts = from_bands(text, n_band)
        if n_band == 2:
            return [text, *texts], texts
        return [lax.psum(text, "band")], texts

    piece_0, tail = direction_parts()
    text = sums(tail, message)
    totals_0, texts = band_totals(text)

    piece_1, tail = direction_parts(text, totals_0, texts)
    totals_1, _ = band_totals(sums(tail, message, text, totals_0))
    pair = gather_rows(jnp.stack([piece_0, piece_1]), bits[-1], n_member, member_pos)
    out = combine(pair, totals_0, totals_1, chunks)
    for bit in reversed(bits[:-1]):
        out = gather_rows(out, bit, n_member, member_pos)
    return out.reshape(levels, lat_rows, lon)


def solution(mesh):
    in_specs = (
        P("member", None, "band", None),
        P(None, "band", None),
        P("member", "band"),
        P("member", "band"),
        P("member", "band"),
        P(),
    )
    out_specs = P(None, "band", None)
    return jax.shard_map(local, mesh=mesh, in_specs=in_specs, out_specs=out_specs, check_vma=False)
```

```python
import functools

import jax
import jax.numpy as jnp
import numpy as np
from jax import lax
from jax.experimental import pallas as pl
from jax.experimental.pallas import tpu as pltpu
from jax.sharding import PartitionSpec as P

HALF = 8
ITERS = 2
REACH = 2 * HALF

huber_edge = 1.5
ensemble_share = 0.75
static_share = 0.25

LANES = 256
GRANT = 20 << 20
F32 = jnp.float32
BF16 = jnp.bfloat16


def tap_matrix(distance, radius):
    offsets = np.arange(-radius, radius + 1).astype(np.float32)
    raw = np.exp(np.float32(-0.5) * (offsets / np.float32(0.5 * radius)) ** 2)
    taps = raw / np.sqrt(np.sum(raw * raw))
    entry = taps[np.clip(distance, -radius, radius) + radius]
    return np.where(np.abs(distance) <= radius, entry, 0.0).astype(np.float32)


def lon_tile(radius):
    source = np.arange(2 * LANES)[:, None] - LANES // 2
    target = np.arange(LANES)[None, :]
    return tap_matrix(source - target, radius)


def lat_block(out_level, out_row, in_level, in_row, rows_total, radius):
    entry = tap_matrix(in_row[None, :] - out_row[:, None], radius)
    inside = (out_row >= 0) & (out_row < rows_total)
    keep = (out_level[:, None] == in_level[None, :]) & inside[:, None]
    return np.where(keep, entry, 0.0)


def lat_operators(levels, rows, bands, radius):
    reach = 2 * radius
    first, second = [], []
    for band in range(bands):
        base = band * rows
        if bands == 2:
            sides = [(base + rows, base + rows) if band == 0 else (base - reach, base - radius)]
        else:
            sides = [(base - reach, base - radius), (base + rows, base + rows)]

        def row_list(start, width):
            level = np.repeat(np.arange(levels), width)
            return level, np.tile(np.arange(width), levels) + start

        own = row_list(base, rows)
        join = lambda parts: tuple(np.concatenate(p) for p in zip(*parts))
        outer = join([own] + [row_list(s[0], reach) for s in sides])
        inner = join([own] + [row_list(s[1], radius) for s in sides])
        first.append(lat_block(*inner, *outer, rows * bands, radius))
        second.append(lat_block(*own, *inner, rows * bands, radius))
    return np.stack(first), np.stack(second)


def split_bf16(x):
    hi = x.astype(BF16)
    lo = (x - hi.astype(F32)).astype(BF16)
    return hi, lo


def counter(count, width):
    column = lax.broadcasted_iota(jnp.int32, (count, LANES // 2), 0).astype(F32).astype(BF16)
    return jnp.concatenate([column] * (width // (LANES // 2)), axis=1)


def onehot(blk, row, rows, blocks):
    count = counter(rows, row.shape[1])
    one, zero = jnp.ones((), BF16), jnp.zeros((), BF16)
    parts = []
    for b in range(blocks):
        here = jnp.where(blk == b, row, -1).astype(F32).astype(BF16)
        parts.append(jnp.where(count == here, one, zero))
    return jnp.concatenate(parts, axis=0)


def limit():
    return pltpu.CompilerParams(vmem_limit_bytes=GRANT)


def vmem():
    return pl.BlockSpec(memory_space=pltpu.VMEM)


def smem():
    return pl.BlockSpec(memory_space=pltpu.SMEM)


def weigh(at_place, value, error):
    departure = value - at_place
    weight = huber_edge / jnp.maximum(jnp.abs(departure / error), huber_edge)
    share = weight / (error * error)
    return share * departure, share


def prepare_kernel(roots, idx_ref, value_ref, error_ref, out_ref):
    chunks, lon = out_ref.shape[0] // 6, out_ref.shape[1]
    position = lax.axis_index("member")
    first, second = position == roots[0], position == roots[1]
    for c in range(chunks):
        lanes = slice(c * lon, (c + 1) * lon)
        idx = idx_ref[:, lanes].astype(F32)
        value, error = value_ref[:, lanes], error_ref[:, lanes]
        coef, share = weigh(0.0, value, error)
        for k, x in enumerate((idx, coef, share)):
            out_ref[k * chunks + c:k * chunks + c + 1, :] = jnp.where(first, x, 0.0)
        for k, x in enumerate((idx, value, error)):
            k += 3
            out_ref[k * chunks + c:k * chunks + c + 1, :] = jnp.where(second, x, 0.0)


def prepare(roots, index, value, error, lon):
    return pl.pallas_call(
        prepare_kernel,
        out_shape=jax.ShapeDtypeStruct((6 * (index.shape[1] // lon), lon), F32),
        in_specs=[smem(), vmem(), vmem(), vmem()],
        out_specs=vmem(),
        compiler_params=limit(),
        name="prepare",
    )(roots, index, value, error)


def add_onehot(idx, coef, blk, row, acc, blocks):
    lane = (idx % LANES).astype(F32).astype(BF16)
    spot = counter(LANES, idx.shape[1]) == lane
    zero = jnp.zeros((), BF16)
    side = jnp.concatenate([jnp.where(spot, x, zero) for x in split_bf16(coef)], axis=0)
    hot = onehot(blk, row, acc.shape[0] // blocks, blocks)
    acc[...] += lax.dot_general(
        hot, side, (((1,), (1,)), ((), ())), preferred_element_type=F32
    )


def total_of(totals, row):
    value = totals[0][row:row + 1, :1]
    for t in totals[1:]:
        value = value + t[row:row + 1, :1]
    return value


def scale_of(totals, chunks):
    along = total_of(totals, chunks)
    return along / (along + total_of(totals, chunks + 1))


def coefficients(second, message, chunks, text, totals, c):
    row = lambda ref, k: ref[k * chunks + c:k * chunks + c + 1, :]
    if not second:
        return row(message, 0), row(message, 1)
    at_place = scale_of(totals, chunks) * row(text, 0)
    error = row(message, 5)
    coef, _ = weigh(at_place, row(message, 4), jnp.where(error > 0, error, 1.0))
    return row(message, 3), coef


def scatter_kernel(second, rows, lon, near, *refs):
    refs = list(refs)
    start_ref = refs.pop(0) if near is not None else None
    out_ref, acc = refs[-2:]
    message = refs[0]
    text, totals = (refs[1], refs[2:-2]) if second else (None, None)
    chunks = message.shape[0] // 6
    width = out_ref.shape[0]
    acc[...] = jnp.zeros_like(acc)
    for c in range(chunks):
        place, coef = coefficients(second, message, chunks, text, totals, c)
        idx = place.astype(jnp.int32)
        blk = (idx % lon) // LANES
        if near is None:
            row = idx // lon
        else:
            row = (idx // lon) % rows - start_ref[near]
            inside = (row >= 0) & (row < REACH)
            row = jnp.where(inside, (idx // (lon * rows)) * REACH + row, -1)
        add_onehot(idx, coef, blk, row, acc, lon // LANES)
    for b in range(lon // LANES):
        part = acc[b * width:(b + 1) * width, :]
        out_ref[:, b * LANES:(b + 1) * LANES] = part[:, :LANES] + part[:, LANES:]


def scatter_obs(levels, rows, lon, message, text, totals, near=None, starts=None):
    second = text is not None
    width = levels * (rows if near is None else REACH)
    args = [message] + ([text, *totals] if second else [])
    specs = [vmem()] * len(args)
    if near is not None:
        args, specs = [starts] + args, [smem()] + specs
    return pl.pallas_call(
        functools.partial(scatter_kernel, second, rows, lon, near),
        out_shape=jax.ShapeDtypeStruct((width, lon), F32),
        in_specs=specs,
        out_specs=vmem(),
        scratch_shapes=[pltpu.VMEM(((lon // LANES) * width, 2 * LANES), F32)],
        compiler_params=limit(),
        name="scatter_own" if near is None else "scatter_near",
    )(*args)


def lon_pass(x, tile):
    rows, lon = x.shape
    half = LANES // 2
    parts = []
    for j in range(lon // LANES):
        lo, hi = j * LANES - half, (j + 1) * LANES + half
        if lo < 0:
            window = jnp.concatenate([x[:, lon + lo:], x[:, :hi]], axis=1)
        elif hi > lon:
            window = jnp.concatenate([x[:, lo:], x[:, :hi - lon]], axis=1)
        else:
            window = x[:, lo:hi]
        parts.append(window)
    stacked = jnp.concatenate(parts, axis=0)
    y = jnp.dot(stacked, tile, preferred_element_type=F32).astype(BF16)
    return jnp.concatenate([y[j * rows:(j + 1) * rows] for j in range(lon // LANES)], axis=1)


def filter_kernel(share, own_ref, ext_ref, grad_ref, gext_ref, var_ref,
                  tile_ref, lat1_ref, lat2_ref, keep_ref, send_ref, acc_ref):
    step = pl.program_id(0)
    position = lax.axis_index("member")
    own = own_ref[0].astype(F32)
    ext = ext_ref[0].astype(F32)
    mixed = jnp.concatenate(
        [(own * grad_ref[...]).astype(BF16), (ext * gext_ref[...]).astype(BF16)], axis=0
    )
    tile = tile_ref[...]
    first = lon_pass(mixed, tile)
    band = lax.axis_index("band")
    first = jnp.dot(lat1_ref[band], first, preferred_element_type=F32).astype(BF16)
    second = lon_pass(first, tile)
    second = jnp.dot(lat2_ref[band], second, preferred_element_type=F32)
    product = own * second

    @pl.when(step == 0)
    def _():
        acc_ref[...] = product

    @pl.when(step > 0)
    def _():
        acc_ref[...] += product

    @pl.when(step == pl.num_programs(0) - 1)
    def _():
        half = keep_ref.shape[0]
        static = jnp.where(position == 0, static_share, 0.0)
        bit = position % 2
        for ref, start in ((keep_ref, bit * half), (send_ref, (1 - bit) * half)):
            rows = pl.ds(pl.multiple_of(start, half), half)
            ref[...] = share * acc_ref[rows, :] + static * var_ref[rows, :] * grad_ref[rows, :]


def filter_members(share, own, ext, grad, gext, variance, tile, lat1, lat2):
    members, rows, lon = own.shape
    whole = lambda a: pl.BlockSpec(a.shape, lambda i: (0,) * a.ndim)
    half = jax.ShapeDtypeStruct((rows // 2, lon), F32)
    return pl.pallas_call(
        functools.partial(filter_kernel, share),
        grid=(members,),
        out_shape=(half, half),
        in_specs=[
            pl.BlockSpec((1,) + own.shape[1:], lambda i: (i, 0, 0)),
            pl.BlockSpec((1,) + ext.shape[1:], lambda i: (i, 0, 0)),
            whole(grad), whole(gext), whole(variance),
            whole(tile), whole(lat1), whole(lat2),
        ],
        out_specs=(whole(half), whole(half)),
        scratch_shapes=[pltpu.VMEM((rows, lon), F32)],
        compiler_params=limit(),
        name="filter_members",
    )(own, ext, grad, gext, variance, tile, lat1, lat2)


def gather_kernel(which, keep_ref, got_ref, message, next_ref, send_ref):
    position = lax.axis_index("member")
    rows, lon = keep_ref.shape
    chunks = message.shape[0] // 6
    start = (position % 2) * rows
    field = keep_ref[...] + got_ref[...]
    low, high = field[:rows // 2], field[rows // 2:]
    upper = (position // 2) % 2 == 1
    next_ref[...] = jnp.where(upper, high, low)
    send_ref[:rows // 2, :] = jnp.where(upper, low, high)
    blocks = lon // LANES
    stacked = jnp.concatenate(
        [field[:, b * LANES:(b + 1) * LANES] for b in range(blocks)], axis=0
    )
    table = jnp.concatenate(split_bf16(jnp.transpose(stacked)), axis=0)
    for n, place in enumerate(which):
        for c in range(chunks):
            at = place * chunks + c
            idx = message[at:at + 1, :].astype(jnp.int32)
            blk = (idx % lon) // LANES
            row = idx // lon - start
            inside = (row >= 0) & (row < rows)
            hot = onehot(blk, jnp.where(inside, row, -1), rows, blocks)
            found = jnp.dot(table, hot, preferred_element_type=F32)
            found = found[:LANES] + found[LANES:]
            spot = lax.broadcasted_iota(jnp.int32, found.shape, 0) == idx % LANES
            value = jnp.sum(jnp.where(spot, found, 0.0), axis=0, keepdims=True)
            at = rows // 2 + n * chunks + c
            send_ref[at:at + 1, :] = value


def gather_places(which, keep, got, message):
    rows, lon = keep.shape
    tail = len(which) * (message.shape[0] // 6)
    return pl.pallas_call(
        functools.partial(gather_kernel, which),
        out_shape=(
            jax.ShapeDtypeStruct((rows // 2, lon), F32),
            jax.ShapeDtypeStruct((rows // 2 + tail, lon), F32),
        ),
        in_specs=[vmem()] * 3,
        out_specs=(vmem(), vmem()),
        compiler_params=limit(),
        name="gather_places",
    )(keep, got, message)


def sums_kernel(second, *refs):
    tail = refs[0][...] + refs[1][...]
    message, out_ref = refs[2], refs[-1]
    chunks = message.shape[0] // 6
    lon = message.shape[1]
    part = lambda ref, k: ref[k * chunks:(k + 1) * chunks, :]
    total = lambda x: jnp.sum(jnp.sum(x, axis=0, keepdims=True), axis=1, keepdims=True)
    out_ref[...] = jnp.zeros_like(out_ref)
    reached = part(tail, 0)
    if second:
        text, totals = refs[3], refs[4:-1]
        at_place = scale_of(totals, chunks) * part(text, 0)
        coef, share = weigh(at_place, part(message, 4), part(message, 5))
        along = total(coef * (reached - at_place))
        curve = total(coef * at_place) + total(share * reached * reached)
    else:
        out_ref[:chunks, :] = part(tail, 1)
        along = total(part(message, 1) * reached)
        curve = total(part(message, 2) * reached * reached)
    out_ref[chunks:chunks + 1, :] = jnp.broadcast_to(along, (1, out_ref.shape[1]))
    out_ref[chunks + 1:chunks + 2, :] = jnp.broadcast_to(curve, (1, out_ref.shape[1]))


def sums(tails, message, text=None, totals=()):
    chunks, lon = message.shape[0] // 6, message.shape[1]
    second = text is not None
    args = [*tails, message] + ([text, *totals] if second else [])
    rows = -(-(chunks + 2) // 8) * 8
    return pl.pallas_call(
        functools.partial(sums_kernel, second),
        out_shape=jax.ShapeDtypeStruct((rows, LANES // 2 if second else lon), F32),
        in_specs=[vmem()] * len(args),
        out_specs=vmem(),
        compiler_params=limit(),
        name="sums",
    )(*args)


def combine_kernel(chunks, count, *refs):
    pair, out_ref = refs[0], refs[-1]
    first, second = refs[1:1 + count], refs[1 + count:-1]
    scale_0 = scale_of(first, chunks)
    scale_1 = scale_of(second, chunks)
    out_ref[...] = scale_0 * pair[0] + scale_1 * pair[1]


def combine(pair, first, second, chunks):
    args = [pair, *first, *second]
    return pl.pallas_call(
        functools.partial(combine_kernel, chunks, len(first)),
        out_shape=jax.ShapeDtypeStruct(pair.shape[1:], F32),
        in_specs=[vmem()] * len(args),
        out_specs=vmem(),
        compiler_params=limit(),
        name="combine",
    )(*args)


def partner(count, bit):
    return [(j, j ^ bit) for j in range(count)]


def member_bits(count):
    bits, d = [], 1
    while d < count:
        bits.append(d)
        d *= 2
    assert d == count
    return bits


def swap(x, bit, count):
    return lax.ppermute(x, "member", partner(count, bit))


def reduce_with_tail(keep, send, bits, count, position):
    rows = keep.shape[0]
    for n, bit in enumerate(bits):
        got = swap(send, bit, count)
        x = keep + got[:rows]
        tail = send[rows:] + got[rows:]
        if n + 1 < len(bits):
            rows //= 2
            upper = (position // bits[n + 1]) % 2 == 1
            keep = jnp.where(upper, x[rows:], x[:rows])
            send = jnp.concatenate([jnp.where(upper, x[:rows], x[rows:]), tail], axis=0)
    return x, tail


def gather_rows(x, bit, count, position):
    other = swap(x, bit, count)
    upper = (position // bit) % 2 == 1
    axis = x.ndim - 2
    return jnp.concatenate([jnp.where(upper, other, x), jnp.where(upper, x, other)], axis=axis)


def from_bands(x, count):
    if count == 2:
        return [lax.ppermute(x, "band", [(0, 1), (1, 0)])]
    up = [(i, i + 1) for i in range(count - 1)]
    down = [(j, i) for i, j in up]
    return [lax.ppermute(x, "band", up), lax.ppermute(x, "band", down)]


def band_halo(ens, count, position):
    rows = ens.shape[2]
    first, last = ens[:, :, :REACH], ens[:, :, rows - REACH:]
    if count == 2:
        edge = jnp.where(position == 0, last, first)
        return [lax.ppermute(edge, "band", [(0, 1), (1, 0)])]
    up = [(i, i + 1) for i in range(count - 1)]
    down = [(j, i) for i, j in up]
    return [lax.ppermute(last, "band", up), lax.ppermute(first, "band", down)]


def local(ensemble, variance, obs_index, obs_value, obs_error, root_ranks):
    members_here, levels, lat_rows, lon = ensemble.shape
    n_member, n_band = lax.axis_size("member"), lax.axis_size("band")
    member_pos, band_pos = lax.axis_index("member"), lax.axis_index("band")
    members = members_here * n_member
    chunks = obs_index.shape[1] // lon
    bits = member_bits(n_member)

    if n_band == 2:
        starts = jnp.where(band_pos == 0, 0, lat_rows - REACH).reshape(1)
    else:
        starts = jnp.array([lat_rows - REACH, 0])
    starts = starts.astype(jnp.int32)
    lat1, lat2 = (jnp.asarray(m, BF16) for m in lat_operators(levels, lat_rows, n_band, HALF))
    tile = jnp.asarray(lon_tile(HALF), BF16)

    message = prepare(root_ranks, obs_index, obs_value, obs_error, lon)
    message = message + swap(message, bits[0], n_member)
    ensemble, message = lax.optimization_barrier((ensemble, message))
    halo = band_halo(ensemble, n_band, band_pos)
    for bit in bits[1:]:
        message = message + swap(message, bit, n_member)
    around = from_bands(message, n_band)

    own = ensemble.reshape(members_here, levels * lat_rows, lon)
    ext = jnp.concatenate([h.reshape(members_here, levels * REACH, lon) for h in halo], axis=1)
    variance = variance.reshape(levels * lat_rows, lon)
    share = ensemble_share / (members - 1)

    def direction_parts(text=None, totals=(), texts=()):
        scatter = functools.partial(scatter_obs, levels, lat_rows, lon)
        grad = scatter(message, text, totals)
        gext = [
            scatter(a, texts[s] if texts else None, totals, s, starts)
            for s, a in enumerate(around)
        ]
        gext = jnp.concatenate(gext, axis=0)
        keep, send = filter_members(share, own, ext, grad, gext, variance, tile, lat1, lat2)
        got = swap(send, bits[0], n_member)
        which = (3,) if texts else (0, 3)
        keep, send = gather_places(which, keep, got, message)
        piece, tail = reduce_with_tail(keep, send, bits[1:], n_member, member_pos)
        return piece, (tail, swap(tail, bits[0], n_member))

    def band_totals(text):
        texts = from_bands(text, n_band)
        if n_band == 2:
            return [text, *texts], texts
        return [lax.psum(text, "band")], texts

    piece_0, tail = direction_parts()
    text = sums(tail, message)
    totals_0, texts = band_totals(text)

    piece_1, tail = direction_parts(text, totals_0, texts)
    totals_1, _ = band_totals(sums(tail, message, text, totals_0))
    pair = gather_rows(jnp.stack([piece_0, piece_1]), bits[-1], n_member, member_pos)
    out = combine(pair, totals_0, totals_1, chunks)
    for bit in reversed(bits[:-1]):
        out = gather_rows(out, bit, n_member, member_pos)
    return out.reshape(levels, lat_rows, lon)


def solution(mesh):
    in_specs = (
        P("member", None, "band", None),
        P(None, "band", None),
        P("member", "band"),
        P("member", "band"),
        P("member", "band"),
        P(),
    )
    out_specs = P(None, "band", None)
    return jax.shard_map(local, mesh=mesh, in_specs=in_specs, out_specs=out_specs, check_vma=False)
```

```python
import functools

import jax
import jax.numpy as jnp
import numpy as np
from jax import lax
from jax.experimental import pallas as pl
from jax.experimental.pallas import tpu as pltpu
from jax.sharding import PartitionSpec as P

HALF = 8
ITERS = 2
REACH = 2 * HALF

huber_edge = 1.5
ensemble_share = 0.75
static_share = 0.25

LANES = 256
MIB = 1 << 20
GROUP = 4
F32 = jnp.float32
BF16 = jnp.bfloat16


def tap_matrix(distance, radius):
    offsets = np.arange(-radius, radius + 1).astype(np.float32)
    raw = np.exp(np.float32(-0.5) * (offsets / np.float32(0.5 * radius)) ** 2)
    taps = raw / np.sqrt(np.sum(raw * raw))
    entry = taps[np.clip(distance, -radius, radius) + radius]
    return np.where(np.abs(distance) <= radius, entry, 0.0).astype(np.float32)


def lon_tile(radius):
    source = np.arange(2 * LANES)[:, None] - LANES // 2
    target = np.arange(LANES)[None, :]
    return tap_matrix(source - target, radius)


def lat_block(out_level, out_row, in_level, in_row, rows_total, radius):
    entry = tap_matrix(in_row[None, :] - out_row[:, None], radius)
    inside = (out_row >= 0) & (out_row < rows_total)
    keep = (out_level[:, None] == in_level[None, :]) & inside[:, None]
    return np.where(keep, entry, 0.0)


def lat_operators(levels, rows, bands, radius):
    reach = 2 * radius
    first, second = [], []
    for band in range(bands):
        base = band * rows
        if bands == 2:
            sides = [(base + rows, base + rows) if band == 0 else (base - reach, base - radius)]
        else:
            sides = [(base - reach, base - radius), (base + rows, base + rows)]

        def row_list(start, width):
            level = np.repeat(np.arange(levels), width)
            return level, np.tile(np.arange(width), levels) + start

        own = row_list(base, rows)
        join = lambda parts: tuple(np.concatenate(p) for p in zip(*parts))
        outer = join([own] + [row_list(s[0], reach) for s in sides])
        inner = join([own] + [row_list(s[1], radius) for s in sides])
        first.append(lat_block(*inner, *outer, rows * bands, radius))
        second.append(lat_block(*own, *inner, rows * bands, radius))
    return np.stack(first), np.stack(second)


def split_bf16(x):
    hi = x.astype(BF16)
    lo = (x - hi.astype(F32)).astype(BF16)
    return hi, lo


def counter(count, width):
    column = lax.broadcasted_iota(jnp.int32, (count, LANES // 2), 0).astype(F32).astype(BF16)
    return jnp.concatenate([column] * (width // (LANES // 2)), axis=1)


def onehot(blk, row, rows, blocks):
    count = counter(rows, row.shape[1])
    one, zero = jnp.ones((), BF16), jnp.zeros((), BF16)
    parts = []
    for b in range(blocks):
        here = jnp.where(blk == b, row, -1).astype(F32).astype(BF16)
        parts.append(jnp.where(count == here, one, zero))
    return jnp.concatenate(parts, axis=0)


def limit(mebibytes):
    return pltpu.CompilerParams(vmem_limit_bytes=mebibytes * MIB)


def vmem():
    return pl.BlockSpec(memory_space=pltpu.VMEM)


def smem():
    return pl.BlockSpec(memory_space=pltpu.SMEM)


def weigh(at_place, value, error):
    departure = value - at_place
    weight = huber_edge / jnp.maximum(jnp.abs(departure / error), huber_edge)
    share = weight / (error * error)
    return share * departure, share


def prepare_kernel(roots, idx_ref, value_ref, error_ref, out_ref):
    chunks, lon = out_ref.shape[0] // 6, out_ref.shape[1]
    position = lax.axis_index("member")
    first, second = position == roots[0], position == roots[1]
    for c in range(chunks):
        lanes = slice(c * lon, (c + 1) * lon)
        idx = idx_ref[:, lanes].astype(F32)
        value, error = value_ref[:, lanes], error_ref[:, lanes]
        coef, share = weigh(0.0, value, error)
        for k, x in enumerate((idx, coef, share)):
            out_ref[k * chunks + c:k * chunks + c + 1, :] = jnp.where(first, x, 0.0)
        for k, x in enumerate((idx, value, error)):
            k += 3
            out_ref[k * chunks + c:k * chunks + c + 1, :] = jnp.where(second, x, 0.0)


def prepare(roots, index, value, error, lon):
    return pl.pallas_call(
        prepare_kernel,
        out_shape=jax.ShapeDtypeStruct((6 * (index.shape[1] // lon), lon), F32),
        in_specs=[smem(), vmem(), vmem(), vmem()],
        out_specs=vmem(),
        name="prepare",
    )(roots, index, value, error)


def add_onehot(idx, coef, blk, row, acc, blocks):
    lane = (idx % LANES).astype(F32).astype(BF16)
    spot = counter(LANES, idx.shape[1]) == lane
    zero = jnp.zeros((), BF16)
    side = jnp.concatenate([jnp.where(spot, x, zero) for x in split_bf16(coef)], axis=0)
    hot = onehot(blk, row, acc.shape[0] // blocks, blocks)
    acc[...] += lax.dot_general(
        hot, side, (((1,), (1,)), ((), ())), preferred_element_type=F32
    )


def total_of(totals, row):
    value = totals[0][row:row + 1, :1]
    for t in totals[1:]:
        value = value + t[row:row + 1, :1]
    return value


def scale_of(totals, chunks):
    along = total_of(totals, chunks)
    return along / (along + total_of(totals, chunks + 1))


def coefficients(second, message, chunks, text, totals, c):
    row = lambda ref, k: ref[k * chunks + c:k * chunks + c + 1, :]
    if not second:
        return row(message, 0), row(message, 1)
    at_place = scale_of(totals, chunks) * row(text, 0)
    error = row(message, 5)
    coef, _ = weigh(at_place, row(message, 4), jnp.where(error > 0, error, 1.0))
    return row(message, 3), coef


def scatter_kernel(second, rows, lon, near, *refs):
    refs = list(refs)
    start_ref = refs.pop(0) if near is not None else None
    out_ref, acc = refs[-2:]
    message = refs[0]
    text, totals = (refs[1], refs[2:-2]) if second else (None, None)
    chunks = message.shape[0] // 6
    width = out_ref.shape[0]
    acc[...] = jnp.zeros_like(acc)
    for c in range(chunks):
        place, coef = coefficients(second, message, chunks, text, totals, c)
        idx = place.astype(jnp.int32)
        blk = (idx % lon) // LANES
        if near is None:
            row = idx // lon
        else:
            row = (idx // lon) % rows - start_ref[near]
            inside = (row >= 0) & (row < REACH)
            row = jnp.where(inside, (idx // (lon * rows)) * REACH + row, -1)
        add_onehot(idx, coef, blk, row, acc, lon // LANES)
    for b in range(lon // LANES):
        part = acc[b * width:(b + 1) * width, :]
        out_ref[:, b * LANES:(b + 1) * LANES] = part[:, :LANES] + part[:, LANES:]


def scatter_obs(levels, rows, lon, message, text, totals, near=None, starts=None):
    second = text is not None
    width = levels * (rows if near is None else REACH)
    args = [message] + ([text, *totals] if second else [])
    specs = [vmem()] * len(args)
    if near is not None:
        args, specs = [starts] + args, [smem()] + specs
    return pl.pallas_call(
        functools.partial(scatter_kernel, second, rows, lon, near),
        out_shape=jax.ShapeDtypeStruct((width, lon), F32),
        in_specs=specs,
        out_specs=vmem(),
        scratch_shapes=[pltpu.VMEM(((lon // LANES) * width, 2 * LANES), F32)],
        compiler_params=limit(8),
        name="scatter_own" if near is None else "scatter_near",
    )(*args)


def lon_pass(x, tile):
    rows, lon = x.shape
    half = LANES // 2
    parts = []
    for j in range(lon // LANES):
        lo, hi = j * LANES - half, (j + 1) * LANES + half
        if lo < 0:
            window = jnp.concatenate([x[:, lon + lo:], x[:, :hi]], axis=1)
        elif hi > lon:
            window = jnp.concatenate([x[:, lo:], x[:, :hi - lon]], axis=1)
        else:
            window = x[:, lo:hi]
        parts.append(window)
    stacked = jnp.concatenate(parts, axis=0)
    y = jnp.dot(stacked, tile, preferred_element_type=F32).astype(BF16)
    return jnp.concatenate([y[j * rows:(j + 1) * rows] for j in range(lon // LANES)], axis=1)


def filter_kernel(share, own_ref, ext_ref, grad_ref, gext_ref, tile_ref, var_hbm, lat1_hbm,
                  lat2_hbm, keep_ref, send_ref, acc_ref, var_ref, lat1_ref, lat2_ref, arrived):
    position = lax.axis_index("member")
    band = lax.axis_index("band")
    members = own_ref.shape[0]
    loads = [
        pltpu.make_async_copy(source, target, arrived.at[k])
        for k, (source, target) in enumerate(
            [(lat1_hbm.at[band], lat1_ref), (lat2_hbm.at[band], lat2_ref), (var_hbm, var_ref)]
        )
    ]
    for load in loads:
        load.start()
    size = GROUP if members % GROUP == 0 else 1
    for start in range(0, members, size):
        group = range(start, start + size)
        mixed = [
            jnp.concatenate(
                [
                    (own_ref[m].astype(F32) * grad_ref[...]).astype(BF16),
                    (ext_ref[m].astype(F32) * gext_ref[...]).astype(BF16),
                ],
                axis=0,
            )
            for m in group
        ]
        tile = tile_ref[...]
        first = [lon_pass(x, tile) for x in mixed]
        if start == 0:
            loads[0].wait()
            loads[1].wait()
        lat1, lat2 = lat1_ref[...], lat2_ref[...]
        first = [jnp.dot(lat1, x, preferred_element_type=F32).astype(BF16) for x in first]
        second = [lon_pass(x, tile) for x in first]
        second = [jnp.dot(lat2, x, preferred_element_type=F32) for x in second]
        product = own_ref[group[0]].astype(F32) * second[0]
        for m, x in zip(group[1:], second[1:]):
            product += own_ref[m].astype(F32) * x
        acc_ref[...] = product if start == 0 else acc_ref[...] + product
    loads[2].wait()
    half = keep_ref.shape[0]
    static = jnp.where(position == 0, static_share, 0.0)
    bit = position % 2
    for ref, start in ((keep_ref, bit * half), (send_ref, (1 - bit) * half)):
        rows = pl.ds(pl.multiple_of(start, half), half)
        ref[...] = share * acc_ref[rows, :] + static * var_ref[rows, :] * grad_ref[rows, :]


def filter_members(share, own, ext, grad, gext, variance, tile, lat1, lat2):
    members, rows, lon = own.shape
    half = jax.ShapeDtypeStruct((rows // 2, lon), F32)
    away = pl.BlockSpec(memory_space=pltpu.HBM)
    return pl.pallas_call(
        functools.partial(filter_kernel, share),
        out_shape=(half, half),
        in_specs=[vmem()] * 5 + [away] * 3,
        out_specs=(vmem(), vmem()),
        scratch_shapes=[
            pltpu.VMEM((rows, lon), F32),
            pltpu.VMEM((rows, lon), F32),
            pltpu.VMEM(lat1.shape[1:], BF16),
            pltpu.VMEM(lat2.shape[1:], BF16),
            pltpu.SemaphoreType.DMA((3,)),
        ],
        compiler_params=limit(14),
        name="filter_members",
    )(own, ext, grad, gext, tile, variance, lat1, lat2)


def gather_kernel(which, keep_ref, got_ref, message, next_ref, send_ref):
    position = lax.axis_index("member")
    rows, lon = keep_ref.shape
    chunks = message.shape[0] // 6
    start = (position % 2) * rows
    field = keep_ref[...] + got_ref[...]
    low, high = field[:rows // 2], field[rows // 2:]
    upper = (position // 2) % 2 == 1
    next_ref[...] = jnp.where(upper, high, low)
    send_ref[:rows // 2, :] = jnp.where(upper, low, high)
    blocks = lon // LANES
    stacked = jnp.concatenate(
        [field[:, b * LANES:(b + 1) * LANES] for b in range(blocks)], axis=0
    )
    table = jnp.concatenate(split_bf16(jnp.transpose(stacked)), axis=0)
    for n, place in enumerate(which):
        for c in range(chunks):
            at = place * chunks + c
            idx = message[at:at + 1, :].astype(jnp.int32)
            blk = (idx % lon) // LANES
            row = idx // lon - start
            inside = (row >= 0) & (row < rows)
            hot = onehot(blk, jnp.where(inside, row, -1), rows, blocks)
            found = jnp.dot(table, hot, preferred_element_type=F32)
            found = found[:LANES] + found[LANES:]
            spot = lax.broadcasted_iota(jnp.int32, found.shape, 0) == idx % LANES
            value = jnp.sum(jnp.where(spot, found, 0.0), axis=0, keepdims=True)
            at = rows // 2 + n * chunks + c
            send_ref[at:at + 1, :] = value


def gather_places(which, keep, got, message):
    rows, lon = keep.shape
    tail = len(which) * (message.shape[0] // 6)
    return pl.pallas_call(
        functools.partial(gather_kernel, which),
        out_shape=(
            jax.ShapeDtypeStruct((rows // 2, lon), F32),
            jax.ShapeDtypeStruct((rows // 2 + tail, lon), F32),
        ),
        in_specs=[vmem()] * 3,
        out_specs=(vmem(), vmem()),
        compiler_params=limit(8),
        name="gather_places",
    )(keep, got, message)


def sums_kernel(second, *refs):
    tail = refs[0][...] + refs[1][...]
    message, out_ref = refs[2], refs[-1]
    chunks = message.shape[0] // 6
    lon = message.shape[1]
    part = lambda ref, k: ref[k * chunks:(k + 1) * chunks, :]
    total = lambda x: jnp.sum(jnp.sum(x, axis=0, keepdims=True), axis=1, keepdims=True)
    out_ref[...] = jnp.zeros_like(out_ref)
    reached = part(tail, 0)
    if second:
        text, totals = refs[3], refs[4:-1]
        at_place = scale_of(totals, chunks) * part(text, 0)
        coef, share = weigh(at_place, part(message, 4), part(message, 5))
        along = total(coef * (reached - at_place))
        curve = total(coef * at_place) + total(share * reached * reached)
    else:
        out_ref[:chunks, :] = part(tail, 1)
        along = total(part(message, 1) * reached)
        curve = total(part(message, 2) * reached * reached)
    out_ref[chunks:chunks + 1, :] = jnp.broadcast_to(along, (1, out_ref.shape[1]))
    out_ref[chunks + 1:chunks + 2, :] = jnp.broadcast_to(curve, (1, out_ref.shape[1]))


def sums(tails, message, text=None, totals=()):
    chunks, lon = message.shape[0] // 6, message.shape[1]
    second = text is not None
    args = [*tails, message] + ([text, *totals] if second else [])
    rows = -(-(chunks + 2) // 8) * 8
    return pl.pallas_call(
        functools.partial(sums_kernel, second),
        out_shape=jax.ShapeDtypeStruct((rows, LANES // 2 if second else lon), F32),
        in_specs=[vmem()] * len(args),
        out_specs=vmem(),
        compiler_params=limit(2),
        name="sums",
    )(*args)


def combine_kernel(chunks, count, *refs):
    pair, out_ref = refs[0], refs[-1]
    first, second = refs[1:1 + count], refs[1 + count:-1]
    scale_0 = scale_of(first, chunks)
    scale_1 = scale_of(second, chunks)
    out_ref[...] = scale_0 * pair[0] + scale_1 * pair[1]


def combine(pair, first, second, chunks):
    args = [pair, *first, *second]
    return pl.pallas_call(
        functools.partial(combine_kernel, chunks, len(first)),
        out_shape=jax.ShapeDtypeStruct(pair.shape[1:], F32),
        in_specs=[vmem()] * len(args),
        out_specs=vmem(),
        compiler_params=limit(2),
        name="combine",
    )(*args)


def partner(count, bit):
    return [(j, j ^ bit) for j in range(count)]


def member_bits(count):
    bits, d = [], 1
    while d < count:
        bits.append(d)
        d *= 2
    assert d == count
    return bits


def swap(x, bit, count):
    return lax.ppermute(x, "member", partner(count, bit))


def reduce_with_tail(keep, send, bits, count, position):
    rows = keep.shape[0]
    for n, bit in enumerate(bits):
        got = swap(send, bit, count)
        x = keep + got[:rows]
        tail = send[rows:] + got[rows:]
        if n + 1 < len(bits):
            rows //= 2
            upper = (position // bits[n + 1]) % 2 == 1
            keep = jnp.where(upper, x[rows:], x[:rows])
            send = jnp.concatenate([jnp.where(upper, x[:rows], x[rows:]), tail], axis=0)
    return x, tail


def gather_rows(x, bit, count, position):
    other = swap(x, bit, count)
    upper = (position // bit) % 2 == 1
    axis = x.ndim - 2
    return jnp.concatenate([jnp.where(upper, other, x), jnp.where(upper, x, other)], axis=axis)


def from_bands(x, count):
    if count == 2:
        return [lax.ppermute(x, "band", [(0, 1), (1, 0)])]
    up = [(i, i + 1) for i in range(count - 1)]
    down = [(j, i) for i, j in up]
    return [lax.ppermute(x, "band", up), lax.ppermute(x, "band", down)]


def band_halo(ens, count, position):
    rows = ens.shape[2]
    first, last = ens[:, :, :REACH], ens[:, :, rows - REACH:]
    if count == 2:
        edge = jnp.where(position == 0, last, first)
        return [lax.ppermute(edge, "band", [(0, 1), (1, 0)])]
    up = [(i, i + 1) for i in range(count - 1)]
    down = [(j, i) for i, j in up]
    return [lax.ppermute(last, "band", up), lax.ppermute(first, "band", down)]


def local(ensemble, variance, obs_index, obs_value, obs_error, root_ranks):
    members_here, levels, lat_rows, lon = ensemble.shape
    n_member, n_band = lax.axis_size("member"), lax.axis_size("band")
    member_pos, band_pos = lax.axis_index("member"), lax.axis_index("band")
    members = members_here * n_member
    chunks = obs_index.shape[1] // lon
    bits = member_bits(n_member)

    if n_band == 2:
        starts = jnp.where(band_pos == 0, 0, lat_rows - REACH).reshape(1)
    else:
        starts = jnp.array([lat_rows - REACH, 0])
    starts = starts.astype(jnp.int32)
    lat1, lat2 = (jnp.asarray(m, BF16) for m in lat_operators(levels, lat_rows, n_band, HALF))
    tile = jnp.asarray(lon_tile(HALF), BF16)

    halo = band_halo(ensemble, n_band, band_pos)
    message = prepare(root_ranks, obs_index, obs_value, obs_error, lon)
    message = message + swap(message, bits[0], n_member)
    for bit in bits[1:]:
        message = message + swap(message, bit, n_member)
    around = from_bands(message, n_band)

    own = ensemble.reshape(members_here, levels * lat_rows, lon)
    ext = jnp.concatenate([h.reshape(members_here, levels * REACH, lon) for h in halo], axis=1)
    variance = variance.reshape(levels * lat_rows, lon)
    share = ensemble_share / (members - 1)

    def direction_parts(text=None, totals=(), texts=()):
        scatter = functools.partial(scatter_obs, levels, lat_rows, lon)
        grad = scatter(message, text, totals)
        gext = [
            scatter(a, texts[s] if texts else None, totals, s, starts)
            for s, a in enumerate(around)
        ]
        gext = jnp.concatenate(gext, axis=0)
        keep, send = filter_members(share, own, ext, grad, gext, variance, tile, lat1, lat2)
        got = swap(send, bits[0], n_member)
        which = (3,) if texts else (0, 3)
        keep, send = gather_places(which, keep, got, message)
        piece, tail = reduce_with_tail(keep, send, bits[1:], n_member, member_pos)
        return piece, (tail, swap(tail, bits[0], n_member))

    def band_totals(text):
        texts = from_bands(text, n_band)
        if n_band == 2:
            return [text, *texts], texts
        return [lax.psum(text, "band")], texts

    piece_0, tail = direction_parts()
    text = sums(tail, message)
    totals_0, texts = band_totals(text)

    piece_1, tail = direction_parts(text, totals_0, texts)
    totals_1, _ = band_totals(sums(tail, message, text, totals_0))
    pair = gather_rows(jnp.stack([piece_0, piece_1]), bits[-1], n_member, member_pos)
    out = combine(pair, totals_0, totals_1, chunks)
    for bit in reversed(bits[:-1]):
        out = gather_rows(out, bit, n_member, member_pos)
    return out.reshape(levels, lat_rows, lon)


def solution(mesh):
    in_specs = (
        P("member", None, "band", None),
        P(None, "band", None),
        P("member", "band"),
        P("member", "band"),
        P("member", "band"),
        P(),
    )
    out_specs = P(None, "band", None)
    return jax.shard_map(local, mesh=mesh, in_specs=in_specs, out_specs=out_specs, check_vma=False)
```

```python
import functools

import jax
import jax.numpy as jnp
import numpy as np
from jax import lax
from jax.experimental import pallas as pl
from jax.experimental.pallas import tpu as pltpu
from jax.sharding import PartitionSpec as P

HALF = 8
ITERS = 2
REACH = 2 * HALF

huber_edge = 1.5
ensemble_share = 0.75
static_share = 0.25

LANES = 256
MIB = 1 << 20
GROUP = 4
F32 = jnp.float32
BF16 = jnp.bfloat16


def tap_matrix(distance, radius):
    offsets = np.arange(-radius, radius + 1).astype(np.float32)
    raw = np.exp(np.float32(-0.5) * (offsets / np.float32(0.5 * radius)) ** 2)
    taps = raw / np.sqrt(np.sum(raw * raw))
    entry = taps[np.clip(distance, -radius, radius) + radius]
    return np.where(np.abs(distance) <= radius, entry, 0.0).astype(np.float32)


def lon_tile(radius):
    source = np.arange(2 * LANES)[:, None] - LANES // 2
    target = np.arange(LANES)[None, :]
    return tap_matrix(source - target, radius)


def lat_block(out_level, out_row, in_level, in_row, rows_total, radius):
    entry = tap_matrix(in_row[None, :] - out_row[:, None], radius)
    inside = (out_row >= 0) & (out_row < rows_total)
    keep = (out_level[:, None] == in_level[None, :]) & inside[:, None]
    return np.where(keep, entry, 0.0)


def lat_operators(levels, rows, bands, radius):
    reach = 2 * radius
    first, second = [], []
    for band in range(bands):
        base = band * rows
        if bands == 2:
            sides = [(base + rows, base + rows) if band == 0 else (base - reach, base - radius)]
        else:
            sides = [(base - reach, base - radius), (base + rows, base + rows)]

        def row_list(start, width):
            level = np.repeat(np.arange(levels), width)
            return level, np.tile(np.arange(width), levels) + start

        own = row_list(base, rows)
        join = lambda parts: tuple(np.concatenate(p) for p in zip(*parts))
        outer = join([own] + [row_list(s[0], reach) for s in sides])
        inner = join([own] + [row_list(s[1], radius) for s in sides])
        first.append(lat_block(*inner, *outer, rows * bands, radius))
        second.append(lat_block(*own, *inner, rows * bands, radius))
    return np.stack(first), np.stack(second)


def split_bf16(x):
    hi = x.astype(BF16)
    lo = (x - hi.astype(F32)).astype(BF16)
    return hi, lo


def counter(count, width):
    column = lax.broadcasted_iota(jnp.int32, (count, LANES // 2), 0).astype(F32).astype(BF16)
    return jnp.concatenate([column] * (width // (LANES // 2)), axis=1)


def onehot(blk, row, rows, blocks):
    count = counter(rows, row.shape[1])
    one, zero = jnp.ones((), BF16), jnp.zeros((), BF16)
    parts = []
    for b in range(blocks):
        here = jnp.where(blk == b, row, -1).astype(F32).astype(BF16)
        parts.append(jnp.where(count == here, one, zero))
    return jnp.concatenate(parts, axis=0)


def limit(mebibytes):
    return pltpu.CompilerParams(vmem_limit_bytes=mebibytes * MIB)


def vmem():
    return pl.BlockSpec(memory_space=pltpu.VMEM)


def weigh(at_place, value, error):
    departure = value - at_place
    weight = huber_edge / jnp.maximum(jnp.abs(departure / error), huber_edge)
    share = weight / (error * error)
    return share * departure, share


def prepare_kernel(bands, bits, root_hbm, ens_hbm, idx_hbm, value_hbm, error_hbm, out_ref,
                   flag_ref, *refs):
    edges, (roots, idx_ref, value_ref, error_ref, arrived) = refs[:-5], refs[-5:]
    rows = ens_hbm.shape[2]
    chunks, lon = out_ref.shape[0] // 6, out_ref.shape[1]
    if bands == 2:
        starts = [jnp.where(lax.axis_index("band") == 0, rows - REACH, 0)]
    else:
        starts = [rows - REACH, 0]
    pairs = [(idx_hbm, idx_ref), (value_hbm, value_ref), (error_hbm, error_ref)]
    pairs.append((root_hbm, roots))
    for start, edge in zip(starts, edges):
        pairs.append((ens_hbm.at[:, :, pl.ds(pl.multiple_of(start, REACH), REACH), :], edge))
    loads = [pltpu.make_async_copy(x, y, arrived.at[k]) for k, (x, y) in enumerate(pairs)]
    for load in loads:
        load.start()
    position = lax.axis_index("member")
    for k in range(flag_ref.shape[0]):
        value = jnp.where(position == 0, static_share, 0.0)
        if k < len(bits):
            value = ((position // bits[k]) % 2).astype(F32)
        flag_ref[k:k + 1, :] = jnp.full((1, flag_ref.shape[1]), value, F32)
    for load in loads[:4]:
        load.wait()
    first, second = position == roots[0], position == roots[1]
    for c in range(chunks):
        lanes = slice(c * lon, (c + 1) * lon)
        idx = idx_ref[:, lanes].astype(F32)
        value, error = value_ref[:, lanes], error_ref[:, lanes]
        coef, share = weigh(0.0, value, error)
        for k, x in enumerate((idx, coef, share)):
            out_ref[k * chunks + c:k * chunks + c + 1, :] = jnp.where(first, x, 0.0)
        for k, x in enumerate((idx, value, error)):
            k += 3
            out_ref[k * chunks + c:k * chunks + c + 1, :] = jnp.where(second, x, 0.0)
    for load in loads[4:]:
        load.wait()


def prepare(bands, bits, roots, ensemble, index, value, error, lon):
    count = 1 if bands == 2 else 2
    away = pl.BlockSpec(memory_space=pl.ANY)
    assert len(bits) < 8
    inputs = [roots, ensemble, index, value, error]
    inputs = [pltpu.with_memory_space_constraint(x, pltpu.HBM) for x in inputs]
    edge = jax.ShapeDtypeStruct(ensemble.shape[:2] + (REACH, lon), BF16)
    return pl.pallas_call(
        functools.partial(prepare_kernel, bands, bits),
        out_shape=(
            jax.ShapeDtypeStruct((6 * (index.shape[1] // lon), lon), F32),
            jax.ShapeDtypeStruct((8, lon), F32),
            *[edge] * count,
        ),
        in_specs=[away] * 5,
        out_specs=[vmem()] * (2 + count),
        scratch_shapes=[
            pltpu.SMEM(roots.shape, roots.dtype),
            pltpu.VMEM(index.shape, index.dtype),
            pltpu.VMEM(index.shape, F32),
            pltpu.VMEM(index.shape, F32),
            pltpu.SemaphoreType.DMA((4 + count,)),
        ],
        compiler_params=limit(8),
        name="prepare",
    )(*inputs)


def add_onehot(idx, coef, row, acc, blocks, lanes):
    blk = (idx % (blocks * lanes)) // lanes
    lane = (idx % lanes).astype(F32).astype(BF16)
    spot = counter(lanes, idx.shape[1]) == lane
    zero = jnp.zeros((), BF16)
    side = jnp.concatenate([jnp.where(spot, x, zero) for x in split_bf16(coef)], axis=0)
    hot = onehot(blk, row, acc.shape[0] // blocks, blocks)
    acc[...] += lax.dot_general(
        hot, side, (((1,), (1,)), ((), ())), preferred_element_type=F32
    )


def total_of(totals, row):
    value = totals[0][row:row + 1, :1]
    for t in totals[1:]:
        value = value + t[row:row + 1, :1]
    return value


def scale_of(totals, chunks):
    along = total_of(totals, chunks)
    return along / (along + total_of(totals, chunks + 1))


def coefficients(second, message, chunks, text, totals, c):
    row = lambda ref, k: ref[k * chunks + c:k * chunks + c + 1, :]
    if not second:
        return row(message, 0), row(message, 1)
    at_place = scale_of(totals, chunks) * row(text, 0)
    error = row(message, 5)
    coef, _ = weigh(at_place, row(message, 4), jnp.where(error > 0, error, 1.0))
    return row(message, 3), coef


def scatter_kernel(second, rows, lon, bands, near, *refs):
    if near is not None:
        start = [rows - REACH, 0][near]
        if bands == 2:
            start = jnp.where(lax.axis_index("band") == 0, 0, rows - REACH)
    out_ref, acc = refs[-2:]
    message = refs[0]
    text, totals = (refs[1], refs[2:-2]) if second else (None, None)
    chunks = message.shape[0] // 6
    width = out_ref.shape[0]
    acc[...] = jnp.zeros_like(acc)
    lanes = acc.shape[1] // 2
    for c in range(chunks):
        place, coef = coefficients(second, message, chunks, text, totals, c)
        idx = place.astype(jnp.int32)
        if near is None:
            row = idx // lon
        else:
            row = (idx // lon) % rows - start
            inside = (row >= 0) & (row < REACH)
            row = jnp.where(inside, (idx // (lon * rows)) * REACH + row, -1)
        add_onehot(idx, coef, row, acc, lon // lanes, lanes)
    for b in range(lon // lanes):
        part = acc[b * width:(b + 1) * width, :]
        out_ref[:, b * lanes:(b + 1) * lanes] = part[:, :lanes] + part[:, lanes:]


def scatter_obs(levels, rows, lon, bands, message, text, totals, near=None):
    second = text is not None
    width = levels * (rows if near is None else REACH)
    lanes = LANES if near is None else LANES // 2
    args = [message] + ([text, *totals] if second else [])
    return pl.pallas_call(
        functools.partial(scatter_kernel, second, rows, lon, bands, near),
        out_shape=jax.ShapeDtypeStruct((width, lon), F32),
        in_specs=[vmem()] * len(args),
        out_specs=vmem(),
        scratch_shapes=[pltpu.VMEM(((lon // lanes) * width, 2 * lanes), F32)],
        compiler_params=limit(8),
        name="scatter_own" if near is None else "scatter_near",
    )(*args)


def lon_pass(x, tile):
    rows, lon = x.shape
    half = LANES // 2
    parts = []
    for j in range(lon // LANES):
        lo, hi = j * LANES - half, (j + 1) * LANES + half
        if lo < 0:
            window = jnp.concatenate([x[:, lon + lo:], x[:, :hi]], axis=1)
        elif hi > lon:
            window = jnp.concatenate([x[:, lo:], x[:, :hi - lon]], axis=1)
        else:
            window = x[:, lo:hi]
        parts.append(window)
    stacked = jnp.concatenate(parts, axis=0)
    y = jnp.dot(stacked, tile, preferred_element_type=F32).astype(BF16)
    return jnp.concatenate([y[j * rows:(j + 1) * rows] for j in range(lon // LANES)], axis=1)


def filter_kernel(share, shapes, own_ref, ext_ref, grad_ref, gext_ref, var_ref, table_ref,
                  keep_ref, send_ref, acc_ref):
    position = lax.axis_index("member")
    band = lax.axis_index("band")
    members = own_ref.shape[0]
    (rows_1, cols_1), (rows_2, cols_2), bands = shapes
    tile = table_ref[:2 * LANES, :LANES]
    start_1 = pl.multiple_of(2 * LANES + band * rows_1, 16)
    start_2 = pl.multiple_of(2 * LANES + bands * rows_1 + band * rows_2, 16)
    lat1 = table_ref[pl.ds(start_1, rows_1), :cols_1]
    lat2 = table_ref[pl.ds(start_2, rows_2), :cols_2]
    size = GROUP if members % GROUP == 0 else 1
    for start in range(0, members, size):
        group = range(start, start + size)
        mixed = [
            jnp.concatenate(
                [
                    (own_ref[m].astype(F32) * grad_ref[...]).astype(BF16),
                    (ext_ref[m].astype(F32) * gext_ref[...]).astype(BF16),
                ],
                axis=0,
            )
            for m in group
        ]
        first = [lon_pass(x, tile) for x in mixed]
        first = [jnp.dot(lat1, x, preferred_element_type=F32).astype(BF16) for x in first]
        second = [lon_pass(x, tile) for x in first]
        second = [jnp.dot(lat2, x, preferred_element_type=F32) for x in second]
        product = own_ref[group[0]].astype(F32) * second[0]
        for m, x in zip(group[1:], second[1:]):
            product += own_ref[m].astype(F32) * x
        acc_ref[...] = product if start == 0 else acc_ref[...] + product
    half = keep_ref.shape[0]
    bit = position % 2
    for ref, start in ((keep_ref, bit * half), (send_ref, (1 - bit) * half)):
        rows = pl.ds(pl.multiple_of(start, half), half)
        ref[...] = share * acc_ref[rows, :] + var_ref[rows, :] * grad_ref[rows, :]


def filter_members(share, shapes, own, ext, grad, gext, static, table):
    members, rows, lon = own.shape
    half = jax.ShapeDtypeStruct((rows // 2, lon), F32)
    return pl.pallas_call(
        functools.partial(filter_kernel, share, shapes),
        out_shape=(half, half),
        in_specs=[vmem()] * 6,
        out_specs=(vmem(), vmem()),
        scratch_shapes=[pltpu.VMEM((rows, lon), F32)],
        compiler_params=limit(14),
        name="filter_members",
    )(own, ext, grad, gext, static, table)


def gather_kernel(which, field_ref, message, out_ref):
    rows, lon = field_ref.shape
    chunks = message.shape[0] // 6
    start = (lax.axis_index("member") % 2) * rows
    field = field_ref[...]
    blocks = lon // LANES
    stacked = jnp.concatenate(
        [field[:, b * LANES:(b + 1) * LANES] for b in range(blocks)], axis=0
    )
    table = jnp.concatenate(split_bf16(jnp.transpose(stacked)), axis=0)
    for n, place in enumerate(which):
        for c in range(chunks):
            at = place * chunks + c
            idx = message[at:at + 1, :].astype(jnp.int32)
            blk = (idx % lon) // LANES
            row = idx // lon - start
            inside = (row >= 0) & (row < rows)
            hot = onehot(blk, jnp.where(inside, row, -1), rows, blocks)
            found = jnp.dot(table, hot, preferred_element_type=F32)
            found = found[:LANES] + found[LANES:]
            spot = lax.broadcasted_iota(jnp.int32, found.shape, 0) == idx % LANES
            value = jnp.sum(jnp.where(spot, found, 0.0), axis=0, keepdims=True)
            out_ref[n * chunks + c:n * chunks + c + 1, :] = value


def gather_places(which, field, message):
    tail = len(which) * (message.shape[0] // 6)
    return pl.pallas_call(
        functools.partial(gather_kernel, which),
        out_shape=jax.ShapeDtypeStruct((tail, field.shape[1]), F32),
        in_specs=[vmem()] * 2,
        out_specs=vmem(),
        compiler_params=limit(8),
        name="gather_places",
    )(field, message)


def sums_kernel(second, *refs):
    tail = refs[0][...] + refs[1][...]
    message, out_ref = refs[2], refs[-1]
    chunks = message.shape[0] // 6
    lon = message.shape[1]
    part = lambda ref, k: ref[k * chunks:(k + 1) * chunks, :]
    total = lambda x: jnp.sum(jnp.sum(x, axis=0, keepdims=True), axis=1, keepdims=True)
    out_ref[...] = jnp.zeros_like(out_ref)
    reached = part(tail, 0)
    if second:
        text, totals = refs[3], refs[4:-1]
        at_place = scale_of(totals, chunks) * part(text, 0)
        coef, share = weigh(at_place, part(message, 4), part(message, 5))
        along = total(coef * (reached - at_place))
        curve = total(coef * at_place) + total(share * reached * reached)
    else:
        out_ref[:chunks, :] = part(tail, 1)
        along = total(part(message, 1) * reached)
        curve = total(part(message, 2) * reached * reached)
    out_ref[chunks:chunks + 1, :] = jnp.broadcast_to(along, (1, out_ref.shape[1]))
    out_ref[chunks + 1:chunks + 2, :] = jnp.broadcast_to(curve, (1, out_ref.shape[1]))


def sums(tails, message, text=None, totals=()):
    chunks, lon = message.shape[0] // 6, message.shape[1]
    second = text is not None
    args = [*tails, message] + ([text, *totals] if second else [])
    rows = -(-(chunks + 2) // 8) * 8
    return pl.pallas_call(
        functools.partial(sums_kernel, second),
        out_shape=jax.ShapeDtypeStruct((rows, LANES // 2 if second else lon), F32),
        in_specs=[vmem()] * len(args),
        out_specs=vmem(),
        compiler_params=limit(2),
        name="sums",
    )(*args)


def combine_kernel(chunks, count, *refs):
    pair, out_ref = refs[0], refs[-1]
    first, second = refs[1:1 + count], refs[1 + count:-1]
    scale_0 = scale_of(first, chunks)
    scale_1 = scale_of(second, chunks)
    out_ref[...] = scale_0 * pair[0] + scale_1 * pair[1]


def combine(pair, first, second, chunks):
    args = [pair, *first, *second]
    return pl.pallas_call(
        functools.partial(combine_kernel, chunks, len(first)),
        out_shape=jax.ShapeDtypeStruct(pair.shape[1:], F32),
        in_specs=[vmem()] * len(args),
        out_specs=vmem(),
        compiler_params=limit(2),
        name="combine",
    )(*args)


def partner(count, bit):
    return [(j, j ^ bit) for j in range(count)]


def member_bits(count):
    bits, d = [], 1
    while d < count:
        bits.append(d)
        d *= 2
    assert d == count
    return bits


def swap(x, bit, count):
    return lax.ppermute(x, "member", partner(count, bit))


def halves(x, upper):
    half = x.shape[0] // 2
    return jnp.where(upper, x[half:], x[:half]), jnp.where(upper, x[:half], x[half:])


def reduce_with_tail(x, tail, bits, count, uppers):
    for bit in bits:
        keep, send = halves(x, uppers[bit])
        rows = keep.shape[0]
        got = swap(jnp.concatenate([send, tail], axis=0), bit, count)
        x = keep + got[:rows]
        tail = tail + got[rows:]
    return x, tail


def gather_rows(x, bit, count, upper):
    other = swap(x, bit, count)
    axis = x.ndim - 2
    return jnp.concatenate([jnp.where(upper, other, x), jnp.where(upper, x, other)], axis=axis)


def from_bands(x, count):
    if count == 2:
        return [lax.ppermute(x, "band", [(0, 1), (1, 0)])]
    up = [(i, i + 1) for i in range(count - 1)]
    down = [(j, i) for i, j in up]
    return [lax.ppermute(x, "band", up), lax.ppermute(x, "band", down)]


def band_halo(edges, count):
    if count == 2:
        return [lax.ppermute(edges[0], "band", [(0, 1), (1, 0)])]
    up = [(i, i + 1) for i in range(count - 1)]
    down = [(j, i) for i, j in up]
    return [lax.ppermute(e, "band", pairs) for e, pairs in zip(edges, (up, down))]


def local(ensemble, variance, obs_index, obs_value, obs_error, root_ranks):
    members_here, levels, lat_rows, lon = ensemble.shape
    n_member, n_band = lax.axis_size("member"), lax.axis_size("band")
    members = members_here * n_member
    chunks = obs_index.shape[1] // lon
    bits = member_bits(n_member)

    lat1, lat2 = lat_operators(levels, lat_rows, n_band, HALF)
    shapes = (lat1.shape[1:], lat2.shape[1:], n_band)
    wide = max(LANES, lat1.shape[2])
    parts = [lon_tile(HALF), *lat1, *lat2]
    parts = [np.pad(p, ((0, 0), (0, wide - p.shape[1]))) for p in parts]
    table = jnp.asarray(np.concatenate(parts, axis=0), BF16)

    message, flags, *edges = prepare(
        n_band, bits, root_ranks, ensemble, obs_index, obs_value, obs_error, lon
    )
    halo = band_halo(edges, n_band)
    message = message + swap(message, bits[0], n_member)
    for bit in bits[1:]:
        message = message + swap(message, bit, n_member)
    around = from_bands(message, n_band)

    own = ensemble.reshape(members_here, levels * lat_rows, lon)
    ext = jnp.concatenate([h.reshape(members_here, levels * REACH, lon) for h in halo], axis=1)
    uppers = {bit: flags[k:k + 1] > 0 for k, bit in enumerate(bits)}
    static = flags[-1] * variance
    static = static.reshape(levels * lat_rows, lon)
    share = ensemble_share / (members - 1)

    def direction_parts(text=None, totals=(), texts=()):
        scatter = functools.partial(scatter_obs, levels, lat_rows, lon, n_band)
        grad = scatter(message, text, totals)
        gext = [
            scatter(a, texts[s] if texts else None, totals, s)
            for s, a in enumerate(around)
        ]
        gext = jnp.concatenate(gext, axis=0)
        keep, send = filter_members(share, shapes, own, ext, grad, gext, static, table)
        field = keep + swap(send, bits[0], n_member)
        keep, send = halves(field, uppers[bits[1]])
        piece = keep + swap(send, bits[1], n_member)
        tail = gather_places((3,) if texts else (0, 3), field, message)
        tail = tail + swap(tail, bits[1], n_member)
        piece, tail = reduce_with_tail(piece, tail, bits[2:], n_member, uppers)
        return piece, (tail, swap(tail, bits[0], n_member))

    def band_totals(text):
        texts = from_bands(text, n_band)
        if n_band == 2:
            return [text, *texts], texts
        return [lax.psum(text, "band")], texts

    piece_0, tail = direction_parts()
    text = sums(tail, message)
    totals_0, texts = band_totals(text)

    piece_1, tail = direction_parts(text, totals_0, texts)
    totals_1, _ = band_totals(sums(tail, message, text, totals_0))
    pair = gather_rows(jnp.stack([piece_0, piece_1]), bits[-1], n_member, uppers[bits[-1]])
    out = combine(pair, totals_0, totals_1, chunks)
    for bit in reversed(bits[:-1]):
        out = gather_rows(out, bit, n_member, uppers[bit])
    return out.reshape(levels, lat_rows, lon)


def solution(mesh):
    in_specs = (
        P("member", None, "band", None),
        P(None, "band", None),
        P("member", "band"),
        P("member", "band"),
        P("member", "band"),
        P(),
    )
    out_specs = P(None, "band", None)
    return jax.shard_map(local, mesh=mesh, in_specs=in_specs, out_specs=out_specs, check_vma=False)
```

```python
import functools

import jax
import jax.numpy as jnp
import numpy as np
from jax import lax
from jax.experimental import pallas as pl
from jax.experimental.pallas import tpu as pltpu
from jax.sharding import PartitionSpec as P


HALF = 8
REACH = 2 * HALF

huber_edge = 1.5
ensemble_share = 0.75
static_share = 0.25

LANES = 256
MIB = 1 << 20
GROUP = 8
F32 = jnp.float32
BF16 = jnp.bfloat16


def tap_matrix(distance, radius):
    offsets = np.arange(-radius, radius + 1).astype(np.float32)
    raw = np.exp(np.float32(-0.5) * (offsets / np.float32(0.5 * radius)) ** 2)
    taps = raw / np.sqrt(np.sum(raw * raw))
    entry = taps[np.clip(distance, -radius, radius) + radius]
    return np.where(np.abs(distance) <= radius, entry, 0.0).astype(np.float32)


def lon_tile(radius):
    source = np.arange(2 * LANES)[:, None] - LANES // 2
    target = np.arange(LANES)[None, :]
    return tap_matrix(source - target, radius)


def lat_block(out_level, out_row, in_level, in_row, rows_total, radius):
    entry = tap_matrix(in_row[None, :] - out_row[:, None], radius)
    inside = (out_row >= 0) & (out_row < rows_total)
    keep = (out_level[:, None] == in_level[None, :]) & inside[:, None]
    return np.where(keep, entry, 0.0)


def lat_operators(levels, rows, bands, radius):
    reach = 2 * radius
    first, second = [], []
    for band in range(bands):
        base = band * rows
        if bands == 2:
            sides = [(base + rows, base + rows) if band == 0 else (base - reach, base - radius)]
        else:
            sides = [(base - reach, base - radius), (base + rows, base + rows)]

        def row_list(start, width):
            level = np.repeat(np.arange(levels), width)
            return level, np.tile(np.arange(width), levels) + start

        own = row_list(base, rows)
        join = lambda parts: tuple(np.concatenate(p) for p in zip(*parts))
        outer = join([own] + [row_list(s[0], reach) for s in sides])
        inner = join([own] + [row_list(s[1], radius) for s in sides])
        first.append(lat_block(*inner, *outer, rows * bands, radius))
        second.append(lat_block(*own, *inner, rows * bands, radius))
    return np.stack(first), np.stack(second)


def split_bf16(x):
    hi = x.astype(BF16)
    lo = (x - hi.astype(F32)).astype(BF16)
    return hi, lo


def counter(count, width):
    column = lax.broadcasted_iota(jnp.int32, (count, LANES // 2), 0).astype(F32).astype(BF16)
    return jnp.concatenate([column] * (width // (LANES // 2)), axis=1)


def onehot(blk, row, rows, blocks):
    count = counter(rows, row.shape[1])
    one, zero = jnp.ones((), BF16), jnp.zeros((), BF16)
    parts = []
    for b in range(blocks):
        here = jnp.where(blk == b, row, -1).astype(F32).astype(BF16)
        parts.append(jnp.where(count == here, one, zero))
    return jnp.concatenate(parts, axis=0)


def limit(mebibytes):
    return pltpu.CompilerParams(vmem_limit_bytes=mebibytes * MIB)


def vmem():
    return pl.BlockSpec(memory_space=pltpu.VMEM)


def weigh(at_place, value, error):
    departure = value - at_place
    weight = huber_edge / jnp.maximum(jnp.abs(departure / error), huber_edge)
    share = weight / (error * error)
    return share * departure, share


def halo_groups(members):
    late = members // 4
    return [members - late, late] if late else [members]


def prepare_kernel(bands, bits, root_hbm, ens_hbm, idx_hbm, value_hbm, error_hbm, out_ref,
                   flag_ref, *refs):
    edges, (roots, idx_ref, value_ref, error_ref, arrived) = refs[:-5], refs[-5:]
    rows = ens_hbm.shape[2]
    chunks, lon = out_ref.shape[0] // 6, out_ref.shape[1]
    if bands == 2:
        starts = [jnp.where(lax.axis_index("band") == 0, rows - REACH, 0)]
    else:
        starts = [rows - REACH, 0]
    pairs = [(idx_hbm, idx_ref), (value_hbm, value_ref), (error_hbm, error_ref)]
    pairs.append((root_hbm, roots))
    member = 0
    for k, edge in enumerate(edges):
        side = k % len(starts)
        some = pl.ds(member, edge.shape[0])
        row = pl.ds(pl.multiple_of(starts[side], REACH), REACH)
        pairs.append((ens_hbm.at[some, :, row, :], edge))
        member += edge.shape[0] if side == len(starts) - 1 else 0
    loads = [pltpu.make_async_copy(x, y, arrived.at[k]) for k, (x, y) in enumerate(pairs)]
    for load in loads:
        load.start()
    position = lax.axis_index("member")
    for k in range(flag_ref.shape[0]):
        value = jnp.where(position == 0, static_share, 0.0)
        if k < len(bits):
            value = ((position // bits[k]) % 2).astype(F32)
        flag_ref[k:k + 1, :] = jnp.full((1, flag_ref.shape[1]), value, F32)
    for load in loads[:4]:
        load.wait()
    first, second = position == roots[0], position == roots[1]
    for c in range(chunks):
        lanes = slice(c * lon, (c + 1) * lon)
        idx = idx_ref[:, lanes].astype(F32)
        value, error = value_ref[:, lanes], error_ref[:, lanes]
        coef, share = weigh(0.0, value, error)
        for k, x in enumerate((idx, coef, share)):
            out_ref[k * chunks + c:k * chunks + c + 1, :] = jnp.where(first, x, 0.0)
        for k, x in enumerate((idx, value, error)):
            k += 3
            out_ref[k * chunks + c:k * chunks + c + 1, :] = jnp.where(second, x, 0.0)
    for load in loads[4:]:
        load.wait()


def prepare(bands, bits, roots, ensemble, index, value, error, lon):
    sides = 1 if bands == 2 else 2
    groups = halo_groups(ensemble.shape[0])
    count = sides * len(groups)
    away = pl.BlockSpec(memory_space=pl.ANY)
    assert len(bits) < 8
    inputs = [roots, ensemble, index, value, error]
    inputs = [pltpu.with_memory_space_constraint(x, pltpu.HBM) for x in inputs]
    edges = [
        jax.ShapeDtypeStruct((n, ensemble.shape[1], REACH, lon), BF16)
        for n in groups
        for _ in range(sides)
    ]
    return pl.pallas_call(
        functools.partial(prepare_kernel, bands, bits),
        out_shape=(
            jax.ShapeDtypeStruct((6 * (index.shape[1] // lon), lon), F32),
            jax.ShapeDtypeStruct((8, lon), F32),
            *edges,
        ),
        in_specs=[away] * 5,
        out_specs=[vmem()] * (2 + count),
        scratch_shapes=[
            pltpu.SMEM(roots.shape, roots.dtype),
            pltpu.VMEM(index.shape, index.dtype),
            pltpu.VMEM(index.shape, F32),
            pltpu.VMEM(index.shape, F32),
            pltpu.SemaphoreType.DMA((4 + count,)),
        ],
        compiler_params=limit(8),
        name="prepare",
    )(*inputs)


def add_onehot(idx, coef, row, acc, blocks, lanes):
    blk = (idx % (blocks * lanes)) // lanes
    lane = (idx % lanes).astype(F32).astype(BF16)
    spot = counter(lanes, idx.shape[1]) == lane
    zero = jnp.zeros((), BF16)
    side = jnp.concatenate([jnp.where(spot, x, zero) for x in split_bf16(coef)], axis=0)
    hot = onehot(blk, row, acc.shape[0] // blocks, blocks)
    acc[...] += lax.dot_general(
        hot, side, (((1,), (1,)), ((), ())), preferred_element_type=F32
    )


def total_of(totals, row):
    value = totals[0][row:row + 1, :1]
    for t in totals[1:]:
        value = value + t[row:row + 1, :1]
    return value


def scale_of(totals, chunks):
    along = total_of(totals, chunks)
    return along / (along + total_of(totals, chunks + 1))


def coefficients(second, message, chunks, text, totals, c):
    row = lambda ref, k: ref[k * chunks + c:k * chunks + c + 1, :]
    if not second:
        return row(message, 0), row(message, 1)
    at_place = scale_of(totals, chunks) * row(text, 0)
    error = row(message, 5)
    coef, _ = weigh(at_place, row(message, 4), jnp.where(error > 0, error, 1.0))
    return row(message, 3), coef


def scatter_kernel(second, rows, lon, bands, near, *refs):
    if near is not None:
        start = [rows - REACH, 0][near]
        if bands == 2:
            start = jnp.where(lax.axis_index("band") == 0, 0, rows - REACH)
    out_ref, acc = refs[-2:]
    message = refs[0]
    text, totals = (refs[1], refs[2:-2]) if second else (None, None)
    chunks = message.shape[0] // 6
    width = out_ref.shape[0]
    acc[...] = jnp.zeros_like(acc)
    lanes = acc.shape[1] // 2
    for c in range(chunks):
        place, coef = coefficients(second, message, chunks, text, totals, c)
        idx = place.astype(jnp.int32)
        if near is None:
            row = idx // lon
        else:
            row = (idx // lon) % rows - start
            inside = (row >= 0) & (row < REACH)
            row = jnp.where(inside, (idx // (lon * rows)) * REACH + row, -1)
        add_onehot(idx, coef, row, acc, lon // lanes, lanes)
    for b in range(lon // lanes):
        part = acc[b * width:(b + 1) * width, :]
        out_ref[:, b * lanes:(b + 1) * lanes] = part[:, :lanes] + part[:, lanes:]


def scatter_obs(levels, rows, lon, bands, message, text, totals, near=None):
    second = text is not None
    width = levels * (rows if near is None else REACH)
    lanes = LANES if near is None else LANES // 2
    args = [message] + ([text, *totals] if second else [])
    return pl.pallas_call(
        functools.partial(scatter_kernel, second, rows, lon, bands, near),
        out_shape=jax.ShapeDtypeStruct((width, lon), F32),
        in_specs=[vmem()] * len(args),
        out_specs=vmem(),
        scratch_shapes=[pltpu.VMEM(((lon // lanes) * width, 2 * lanes), F32)],
        compiler_params=limit(8),
        name="scatter_own" if near is None else "scatter_near",
    )(*args)


def lon_pass(x, tile):
    rows, lon = x.shape
    half = LANES // 2
    parts = []
    for j in range(lon // LANES):
        lo, hi = j * LANES - half, (j + 1) * LANES + half
        if lo < 0:
            window = jnp.concatenate([x[:, lon + lo:], x[:, :hi]], axis=1)
        elif hi > lon:
            window = jnp.concatenate([x[:, lo:], x[:, :hi - lon]], axis=1)
        else:
            window = x[:, lo:hi]
        parts.append(window)
    stacked = jnp.concatenate(parts, axis=0)
    y = jnp.dot(stacked, tile, preferred_element_type=F32).astype(BF16)
    return jnp.concatenate([y[j * rows:(j + 1) * rows] for j in range(lon // LANES)], axis=1)


def filter_kernel(share, shapes, kept, first_member, resume, finish, *refs):
    own_ref, grad_ref, gext_ref, static_ref, table_ref = refs[:5]
    ext_refs, out_ref = refs[5:-1], refs[-1]
    sum_ref = None
    if resume:
        ext_refs, sum_ref = ext_refs[:-1], ext_refs[-1]
    bit = lax.axis_index("member") % 2
    bit = bit if kept else 1 - bit
    band = lax.axis_index("band")
    near_of = [(ref, k) for ref in ext_refs for k in range(ref.shape[1])]
    members = len(near_of)
    (rows_1, cols_1), (rows_2, cols_2), bands = shapes
    sources = ext_refs[0].shape[0]
    tile = table_ref[:2 * LANES, :LANES]
    start_1 = pl.multiple_of(2 * LANES + band * rows_1, 16)
    start_2 = pl.multiple_of(2 * LANES + bands * rows_1 + band * rows_2, 16)
    lat1 = table_ref[pl.ds(start_1, rows_1), :cols_1]
    lat2 = table_ref[pl.ds(start_2, rows_2), :cols_2]
    rows = own_ref.shape[1] // 2
    near = ext_refs[0].shape[2] // 2
    own_part = pl.ds(pl.multiple_of(bit * rows, rows), rows)
    ext_part = pl.ds(pl.multiple_of(bit * near, near), near)
    grad = grad_ref[own_part, :]
    size = min(GROUP, members)
    for start in range(0, members, size):
        group = range(start, min(start + size, members))
        mixed = []
        for m in group:
            parts = [(own_ref[first_member + m, own_part, :].astype(F32) * grad).astype(BF16)]
            ext_ref, k = near_of[m]
            for s in range(sources):
                ext = ext_ref[s, k, ext_part, :].astype(F32)
                parts.append((ext * gext_ref[s, ext_part, :]).astype(BF16))
            mixed.append(jnp.concatenate(parts, axis=0))
        first = [lon_pass(x, tile) for x in mixed]
        first = [jnp.dot(lat1, x, preferred_element_type=F32).astype(BF16) for x in first]
        second = [lon_pass(x, tile) for x in first]
        second = [jnp.dot(lat2, x, preferred_element_type=F32) for x in second]
        product = own_ref[first_member + group[0], own_part, :].astype(F32) * second[0]
        for m, x in zip(group[1:], second[1:]):
            product += own_ref[first_member + m, own_part, :].astype(F32) * x
        if start > 0:
            product += out_ref[...]
        elif resume:
            product += sum_ref[...]
        if finish and start + size >= members:
            product = share * product + static_ref[own_part, :] * grad
        out_ref[...] = product


def filter_members(share, shapes, kept, first_member, total, own, ext, grad, gext, static, table):
    _, rows, lon = own.shape
    resume = total is not None
    finish = first_member + sum(e.shape[1] for e in ext) == own.shape[0]
    args = [own, grad, gext, static, table, *ext] + ([total] if resume else [])
    kernel = functools.partial(
        filter_kernel, share, shapes, kept, first_member, resume, finish
    )
    return pl.pallas_call(
        kernel,
        out_shape=jax.ShapeDtypeStruct((rows // 2, lon), F32),
        in_specs=[vmem()] * len(args),
        out_specs=vmem(),
        compiler_params=limit(14),
        name="filter_keep" if kept else "filter_send",
    )(*args)


def gather_kernel(which, field_ref, message, out_ref):
    rows, lon = field_ref.shape
    chunks = message.shape[0] // 6
    start = (lax.axis_index("member") % 2) * rows
    field = field_ref[...]
    blocks = lon // LANES
    stacked = jnp.concatenate(
        [field[:, b * LANES:(b + 1) * LANES] for b in range(blocks)], axis=0
    )
    table = jnp.concatenate(split_bf16(jnp.transpose(stacked)), axis=0)
    for n, place in enumerate(which):
        for c in range(chunks):
            at = place * chunks + c
            idx = message[at:at + 1, :].astype(jnp.int32)
            blk = (idx % lon) // LANES
            row = idx // lon - start
            inside = (row >= 0) & (row < rows)
            hot = onehot(blk, jnp.where(inside, row, -1), rows, blocks)
            found = jnp.dot(table, hot, preferred_element_type=F32)
            found = found[:LANES] + found[LANES:]
            spot = lax.broadcasted_iota(jnp.int32, found.shape, 0) == idx % LANES
            value = jnp.sum(jnp.where(spot, found, 0.0), axis=0, keepdims=True)
            out_ref[n * chunks + c:n * chunks + c + 1, :] = value


def gather_places(which, field, message):
    tail = len(which) * (message.shape[0] // 6)
    return pl.pallas_call(
        functools.partial(gather_kernel, which),
        out_shape=jax.ShapeDtypeStruct((tail, field.shape[1]), F32),
        in_specs=[vmem()] * 2,
        out_specs=vmem(),
        compiler_params=limit(8),
        name="gather_places",
    )(field, message)


def sums_kernel(second, *refs):
    tail = refs[0][...] + refs[1][...]
    message, out_ref = refs[2], refs[-1]
    chunks = message.shape[0] // 6
    part = lambda ref, k: ref[k * chunks:(k + 1) * chunks, :]
    total = lambda x: jnp.sum(jnp.sum(x, axis=0, keepdims=True), axis=1, keepdims=True)
    out_ref[...] = jnp.zeros_like(out_ref)
    reached = part(tail, 0)
    if second:
        text, totals = refs[3], refs[4:-1]
        at_place = scale_of(totals, chunks) * part(text, 0)
        coef, share = weigh(at_place, part(message, 4), part(message, 5))
        along = total(coef * (reached - at_place))
        curve = total(coef * at_place) + total(share * reached * reached)
    else:
        out_ref[:chunks, :] = part(tail, 1)
        along = total(part(message, 1) * reached)
        curve = total(part(message, 2) * reached * reached)
    out_ref[chunks:chunks + 1, :] = jnp.broadcast_to(along, (1, out_ref.shape[1]))
    out_ref[chunks + 1:chunks + 2, :] = jnp.broadcast_to(curve, (1, out_ref.shape[1]))


def sums(tails, message, text=None, totals=()):
    chunks, lon = message.shape[0] // 6, message.shape[1]
    second = text is not None
    args = [*tails, message] + ([text, *totals] if second else [])
    rows = -(-(chunks + 2) // 8) * 8
    return pl.pallas_call(
        functools.partial(sums_kernel, second),
        out_shape=jax.ShapeDtypeStruct((rows, LANES // 2 if second else lon), F32),
        in_specs=[vmem()] * len(args),
        out_specs=vmem(),
        compiler_params=limit(2),
        name="sums",
    )(*args)


def combine_kernel(chunks, count, *refs):
    pair, out_ref = refs[0], refs[-1]
    first, second = refs[1:1 + count], refs[1 + count:-1]
    scale_0 = scale_of(first, chunks)
    scale_1 = scale_of(second, chunks)
    out_ref[...] = (scale_0 * pair[0] + scale_1 * pair[1]).astype(out_ref.dtype)


def combine(pair, first, second, chunks):
    args = [pair, *first, *second]
    return pl.pallas_call(
        functools.partial(combine_kernel, chunks, len(first)),
        out_shape=jax.ShapeDtypeStruct(pair.shape[1:], BF16),
        in_specs=[vmem()] * len(args),
        out_specs=vmem(),
        compiler_params=limit(2),
        name="combine",
    )(*args)


def partner(count, bit):
    return [(j, j ^ bit) for j in range(count)]


def member_bits(count):
    bits, d = [], 1
    while d < count:
        bits.append(d)
        d *= 2
    assert d == count
    return bits


def swap(x, bit, count):
    return lax.ppermute(x, "member", partner(count, bit))


def halves(x, upper):
    half = x.shape[0] // 2
    return jnp.where(upper, x[half:], x[:half]), jnp.where(upper, x[:half], x[half:])


def reduce_with_tail(x, tail, bits, count, uppers):
    for bit in bits:
        keep, send = halves(x, uppers[bit])
        rows = keep.shape[0]
        got = swap(jnp.concatenate([send, tail], axis=0), bit, count)
        x = keep + got[:rows]
        tail = tail + got[rows:]
    return x, tail


def reduce_square(x, tail, high, low, count, uppers):
    keep, send = halves(x, uppers[high])
    near, far = halves(keep, uppers[low]), halves(send, uppers[low])
    rows = near[0].shape[0]
    total = jnp.concatenate([near[0], tail], axis=0)
    for part, bit in ((near[1], low), (far[0], high), (far[1], high | low)):
        total = total + swap(jnp.concatenate([part, tail], axis=0), bit, count)
    return total[:rows], total[rows:]


def gather_rows(x, bit, count, upper):
    other = swap(x, bit, count)
    axis = x.ndim - 2
    return jnp.concatenate([jnp.where(upper, other, x), jnp.where(upper, x, other)], axis=axis)


def join_rows(x, other, upper):
    axis = x.ndim - 2
    return jnp.concatenate([jnp.where(upper, other, x), jnp.where(upper, x, other)], axis=axis)


def gather_square(x, high, low, count, uppers):
    across, along, both = (swap(x, bit, count) for bit in (high, low, high | low))
    mine = join_rows(x, along, uppers[low])
    other = join_rows(across, both, uppers[low])
    return join_rows(mine, other, uppers[high])


def from_bands(x, count):
    if count == 2:
        return [lax.ppermute(x, "band", [(0, 1), (1, 0)])]
    up = [(i, i + 1) for i in range(count - 1)]
    down = [(j, i) for i, j in up]
    return [lax.ppermute(x, "band", up), lax.ppermute(x, "band", down)]


def band_halo(edges, count):
    if count == 2:
        return [lax.ppermute(edges[0], "band", [(0, 1), (1, 0)])]
    up = [(i, i + 1) for i in range(count - 1)]
    down = [(j, i) for i, j in up]
    return [lax.ppermute(e, "band", pairs) for e, pairs in zip(edges, (up, down))]


def local(ensemble, variance, obs_index, obs_value, obs_error, root_ranks):
    members_here, levels, lat_rows, lon = ensemble.shape
    n_member, n_band = lax.axis_size("member"), lax.axis_size("band")
    members = members_here * n_member
    chunks = obs_index.shape[1] // lon
    bits = member_bits(n_member)

    lat1, lat2 = lat_operators(levels // 2, lat_rows, n_band, HALF)
    shapes = (lat1.shape[1:], lat2.shape[1:], n_band)
    wide = max(LANES, lat1.shape[2])
    parts = [lon_tile(HALF), *lat1, *lat2]
    parts = [np.pad(p, ((0, 0), (0, wide - p.shape[1]))) for p in parts]
    table = jnp.asarray(np.concatenate(parts, axis=0), BF16)

    message, flags, *edges = prepare(
        n_band, bits, root_ranks, ensemble, obs_index, obs_value, obs_error, lon
    )
    sides = 1 if n_band == 2 else 2
    halo = band_halo(edges[:sides], n_band)
    message = message + swap(message, bits[0], n_member)
    for bit in bits[1:]:
        message = message + swap(message, bit, n_member)
    around = from_bands(message, n_band)

    own = ensemble.reshape(members_here, levels * lat_rows, lon)
    near_rows = lambda part: jnp.stack(
        [h.reshape(h.shape[0], levels * REACH, lon) for h in part]
    )
    ext = [near_rows(halo)]
    uppers = {bit: flags[k:k + 1] > 0 for k, bit in enumerate(bits)}
    static = flags[-1] * variance
    static = static.reshape(levels * lat_rows, lon)
    share = ensemble_share / (members - 1)

    def direction_parts(rest, text=None, totals=(), texts=()):
        scatter = functools.partial(scatter_obs, levels, lat_rows, lon, n_band)
        grad = scatter(message, text, totals)
        gext = [
            scatter(a, texts[s] if texts else None, totals, s)
            for s, a in enumerate(around)
        ]
        filters = functools.partial(filter_members, share, shapes)
        parts = (grad, jnp.stack(gext), static, table)
        if rest:
            early = [filters(kept, 0, None, own, ext, *parts) for kept in (False, True)]
            first = ext[0].shape[1]
            late = band_halo(rest, n_band)
            ext.append(near_rows(late))
            send = filters(False, first, early[0], own, ext[1:], *parts)
            got = swap(send, bits[0], n_member)
            field = filters(True, first, early[1], own, ext[1:], *parts) + got
        else:
            got = swap(filters(False, 0, None, own, ext, *parts), bits[0], n_member)
            field = filters(True, 0, None, own, ext, *parts) + got
        keep, send = halves(field, uppers[bits[1]])
        piece = keep + swap(send, bits[1], n_member)
        tail = gather_places((3,) if texts else (0, 3), field, message)
        tail = tail + swap(tail, bits[1], n_member)
        piece, tail = reduce_square(piece, tail, bits[2], bits[3], n_member, uppers)
        piece, tail = reduce_with_tail(piece, tail, bits[4:], n_member, uppers)
        return piece, (tail, swap(tail, bits[0], n_member))

    def band_totals(text):
        texts = from_bands(text, n_band)
        if n_band == 2:
            return [text, *texts], texts
        return [lax.psum(text, "band")], texts

    piece_0, tail = direction_parts(edges[sides:])
    text = sums(tail, message)
    totals_0, texts = band_totals(text)

    piece_1, tail = direction_parts([], text, totals_0, texts)
    totals_1, _ = band_totals(sums(tail, message, text, totals_0))
    pair = jnp.stack([piece_0, piece_1])
    for bit in bits[:3:-1]:
        pair = gather_rows(pair, bit, n_member, uppers[bit])
    pair = gather_square(pair, bits[2], bits[3], n_member, uppers)
    out = combine(pair, totals_0, totals_1, chunks)
    for bit in (bits[1], bits[0]):
        out = gather_rows(out, bit, n_member, uppers[bit])
    return out.astype(F32).reshape(levels, lat_rows, lon)


def solution(mesh):
    in_specs = (
        P("member", None, "band", None),
        P(None, "band", None),
        P("member", "band"),
        P("member", "band"),
        P("member", "band"),
        P(),
    )
    out_specs = P(None, "band", None)
    return jax.shard_map(local, mesh=mesh, in_specs=in_specs, out_specs=out_specs, check_vma=False)
```

```python
import functools

import jax
import jax.numpy as jnp
import numpy as np
from jax import lax
from jax.experimental import pallas as pl
from jax.experimental.pallas import tpu as pltpu
from jax.sharding import PartitionSpec as P


HALF = 8
REACH = 2 * HALF

huber_edge = 1.5
ensemble_share = 0.75
static_share = 0.25

LANES = 256
MIB = 1 << 20
GROUP = 8
F32 = jnp.float32
BF16 = jnp.bfloat16


def tap_matrix(distance, radius):
    offsets = np.arange(-radius, radius + 1).astype(np.float32)
    raw = np.exp(np.float32(-0.5) * (offsets / np.float32(0.5 * radius)) ** 2)
    taps = raw / np.sqrt(np.sum(raw * raw))
    entry = taps[np.clip(distance, -radius, radius) + radius]
    return np.where(np.abs(distance) <= radius, entry, 0.0).astype(np.float32)


def lon_tile(radius):
    source = np.arange(2 * LANES)[:, None] - LANES // 2
    target = np.arange(LANES)[None, :]
    return tap_matrix(source - target, radius)


def lat_block(out_level, out_row, in_level, in_row, rows_total, radius):
    entry = tap_matrix(in_row[None, :] - out_row[:, None], radius)
    inside = (out_row >= 0) & (out_row < rows_total)
    keep = (out_level[:, None] == in_level[None, :]) & inside[:, None]
    return np.where(keep, entry, 0.0)


def lat_operators(levels, rows, bands, radius):
    reach = 2 * radius
    first, second = [], []
    for band in range(bands):
        base = band * rows
        if bands == 2:
            sides = [(base + rows, base + rows) if band == 0 else (base - reach, base - radius)]
        else:
            sides = [(base - reach, base - radius), (base + rows, base + rows)]

        def row_list(start, width):
            level = np.repeat(np.arange(levels), width)
            return level, np.tile(np.arange(width), levels) + start

        own = row_list(base, rows)
        join = lambda parts: tuple(np.concatenate(p) for p in zip(*parts))
        outer = join([own] + [row_list(s[0], reach) for s in sides])
        inner = join([own] + [row_list(s[1], radius) for s in sides])
        first.append(lat_block(*inner, *outer, rows * bands, radius))
        second.append(lat_block(*own, *inner, rows * bands, radius))
    return np.stack(first), np.stack(second)


def split_bf16(x):
    hi = x.astype(BF16)
    lo = (x - hi.astype(F32)).astype(BF16)
    return hi, lo


def counter(count, width):
    column = lax.broadcasted_iota(jnp.int32, (count, LANES // 2), 0).astype(F32).astype(BF16)
    return jnp.concatenate([column] * (width // (LANES // 2)), axis=1)


def onehot(blk, row, rows, blocks):
    count = counter(rows, row.shape[1])
    one, zero = jnp.ones((), BF16), jnp.zeros((), BF16)
    parts = []
    for b in range(blocks):
        here = jnp.where(blk == b, row, -1).astype(F32).astype(BF16)
        parts.append(jnp.where(count == here, one, zero))
    return jnp.concatenate(parts, axis=0)


def limit(mebibytes):
    return pltpu.CompilerParams(vmem_limit_bytes=mebibytes * MIB)


def vmem():
    return pl.BlockSpec(memory_space=pltpu.VMEM)


def weigh(at_place, value, error):
    departure = value - at_place
    weight = huber_edge / jnp.maximum(jnp.abs(departure / error), huber_edge)
    share = weight / (error * error)
    return share * departure, share


def halo_groups(members):
    late = members // 4
    return [members - late, late] if late else [members]


def prepare_kernel(bands, bits, root_hbm, ens_hbm, idx_hbm, value_hbm, error_hbm, out_ref,
                   flag_ref, *refs):
    edges, (roots, idx_ref, value_ref, error_ref, arrived) = refs[:-5], refs[-5:]
    rows = ens_hbm.shape[2]
    chunks, lon = out_ref.shape[0] // 6, out_ref.shape[1]
    if bands == 2:
        starts = [jnp.where(lax.axis_index("band") == 0, rows - REACH, 0)]
    else:
        starts = [rows - REACH, 0]
    pairs = [(idx_hbm, idx_ref), (value_hbm, value_ref), (error_hbm, error_ref)]
    pairs.append((root_hbm, roots))
    member = 0
    for k, edge in enumerate(edges):
        side = k % len(starts)
        some = pl.ds(member, edge.shape[0])
        row = pl.ds(pl.multiple_of(starts[side], REACH), REACH)
        pairs.append((ens_hbm.at[some, :, row, :], edge))
        member += edge.shape[0] if side == len(starts) - 1 else 0
    loads = [pltpu.make_async_copy(x, y, arrived.at[k]) for k, (x, y) in enumerate(pairs)]
    for load in loads:
        load.start()
    position = lax.axis_index("member")
    for k in range(flag_ref.shape[0]):
        value = jnp.where(position == 0, static_share, 0.0)
        if k < len(bits):
            value = ((position // bits[k]) % 2).astype(F32)
        flag_ref[k:k + 1, :] = jnp.full((1, flag_ref.shape[1]), value, F32)
    for load in loads[:4]:
        load.wait()
    first, second = position == roots[0], position == roots[1]
    for c in range(chunks):
        lanes = slice(c * lon, (c + 1) * lon)
        idx = idx_ref[:, lanes].astype(F32)
        value, error = value_ref[:, lanes], error_ref[:, lanes]
        coef, share = weigh(0.0, value, error)
        for k, x in enumerate((idx, coef, share)):
            out_ref[k * chunks + c:k * chunks + c + 1, :] = jnp.where(first, x, 0.0)
        for k, x in enumerate((idx, value, error)):
            k += 3
            out_ref[k * chunks + c:k * chunks + c + 1, :] = jnp.where(second, x, 0.0)
    for load in loads[4:]:
        load.wait()


def prepare(bands, bits, roots, ensemble, index, value, error, lon):
    sides = 1 if bands == 2 else 2
    groups = halo_groups(ensemble.shape[0])
    count = sides * len(groups)
    away = pl.BlockSpec(memory_space=pl.ANY)
    assert len(bits) < 8
    inputs = [roots, ensemble, index, value, error]
    inputs = [pltpu.with_memory_space_constraint(x, pltpu.HBM) for x in inputs]
    edges = [
        jax.ShapeDtypeStruct((n, ensemble.shape[1], REACH, lon), BF16)
        for n in groups
        for _ in range(sides)
    ]
    return pl.pallas_call(
        functools.partial(prepare_kernel, bands, bits),
        out_shape=(
            jax.ShapeDtypeStruct((6 * (index.shape[1] // lon), lon), F32),
            jax.ShapeDtypeStruct((8, lon), F32),
            *edges,
        ),
        in_specs=[away] * 5,
        out_specs=[vmem()] * (2 + count),
        scratch_shapes=[
            pltpu.SMEM(roots.shape, roots.dtype),
            pltpu.VMEM(index.shape, index.dtype),
            pltpu.VMEM(index.shape, F32),
            pltpu.VMEM(index.shape, F32),
            pltpu.SemaphoreType.DMA((4 + count,)),
        ],
        compiler_params=limit(8),
        name="prepare",
    )(*inputs)


def add_onehot(idx, coef, row, acc, blocks, lanes):
    blk = (idx % (blocks * lanes)) // lanes
    lane = (idx % lanes).astype(F32).astype(BF16)
    spot = counter(lanes, idx.shape[1]) == lane
    zero = jnp.zeros((), BF16)
    side = jnp.concatenate([jnp.where(spot, x, zero) for x in split_bf16(coef)], axis=0)
    hot = onehot(blk, row, acc.shape[0] // blocks, blocks)
    acc[...] += lax.dot_general(
        hot, side, (((1,), (1,)), ((), ())), preferred_element_type=F32
    )


def total_of(totals, row):
    value = totals[0][row:row + 1, :1]
    for t in totals[1:]:
        value = value + t[row:row + 1, :1]
    return value


def scale_of(totals, chunks):
    along = total_of(totals, chunks)
    return along / (along + total_of(totals, chunks + 1))


def coefficients(second, message, chunks, text, totals, c):
    row = lambda ref, k: ref[k * chunks + c:k * chunks + c + 1, :]
    if not second:
        return row(message, 0), row(message, 1)
    at_place = scale_of(totals, chunks) * row(text, 0)
    error = row(message, 5)
    coef, _ = weigh(at_place, row(message, 4), jnp.where(error > 0, error, 1.0))
    return row(message, 3), coef


def scatter_kernel(second, rows, lon, bands, near, *refs):
    if near is not None:
        start = [rows - REACH, 0][near]
        if bands == 2:
            start = jnp.where(lax.axis_index("band") == 0, 0, rows - REACH)
    out_ref, acc = refs[-2:]
    message = refs[0]
    text, totals = (refs[1], refs[2:-2]) if second else (None, None)
    chunks = message.shape[0] // 6
    width = out_ref.shape[0]
    acc[...] = jnp.zeros_like(acc)
    lanes = acc.shape[1] // 2
    for c in range(chunks):
        place, coef = coefficients(second, message, chunks, text, totals, c)
        idx = place.astype(jnp.int32)
        if near is None:
            row = idx // lon
        else:
            row = (idx // lon) % rows - start
            inside = (row >= 0) & (row < REACH)
            row = jnp.where(inside, (idx // (lon * rows)) * REACH + row, -1)
        add_onehot(idx, coef, row, acc, lon // lanes, lanes)
    for b in range(lon // lanes):
        part = acc[b * width:(b + 1) * width, :]
        out_ref[:, b * lanes:(b + 1) * lanes] = part[:, :lanes] + part[:, lanes:]


def scatter_obs(levels, rows, lon, bands, message, text, totals, near=None):
    second = text is not None
    width = levels * (rows if near is None else REACH)
    lanes = LANES if near is None else LANES // 2
    args = [message] + ([text, *totals] if second else [])
    return pl.pallas_call(
        functools.partial(scatter_kernel, second, rows, lon, bands, near),
        out_shape=jax.ShapeDtypeStruct((width, lon), F32),
        in_specs=[vmem()] * len(args),
        out_specs=vmem(),
        scratch_shapes=[pltpu.VMEM(((lon // lanes) * width, 2 * lanes), F32)],
        compiler_params=limit(8),
        name="scatter_own" if near is None else "scatter_near",
    )(*args)


def lon_pass(x, tile):
    rows, lon = x.shape
    half = LANES // 2
    parts = []
    for j in range(lon // LANES):
        lo, hi = j * LANES - half, (j + 1) * LANES + half
        if lo < 0:
            window = jnp.concatenate([x[:, lon + lo:], x[:, :hi]], axis=1)
        elif hi > lon:
            window = jnp.concatenate([x[:, lo:], x[:, :hi - lon]], axis=1)
        else:
            window = x[:, lo:hi]
        parts.append(window)
    stacked = jnp.concatenate(parts, axis=0)
    y = jnp.dot(stacked, tile, preferred_element_type=F32).astype(BF16)
    return jnp.concatenate([y[j * rows:(j + 1) * rows] for j in range(lon // LANES)], axis=1)


def filter_kernel(share, shapes, kept, first_member, resume, finish, *refs):
    own_ref, grad_ref, gext_ref, static_ref, table_ref = refs[:5]
    ext_refs, out_ref = refs[5:-1], refs[-1]
    sum_ref = None
    if resume:
        ext_refs, sum_ref = ext_refs[:-1], ext_refs[-1]
    bit = lax.axis_index("member") % 2
    bit = bit if kept else 1 - bit
    band = lax.axis_index("band")
    near_of = [(ref, k) for ref in ext_refs for k in range(ref.shape[1])]
    members = len(near_of)
    (rows_1, cols_1), (rows_2, cols_2), bands = shapes
    sources = ext_refs[0].shape[0]
    tile = table_ref[:2 * LANES, :LANES]
    start_1 = pl.multiple_of(2 * LANES + band * rows_1, 16)
    start_2 = pl.multiple_of(2 * LANES + bands * rows_1 + band * rows_2, 16)
    lat1 = table_ref[pl.ds(start_1, rows_1), :cols_1]
    lat2 = table_ref[pl.ds(start_2, rows_2), :cols_2]
    rows = own_ref.shape[1] // 2
    near = ext_refs[0].shape[2] // 2
    own_part = pl.ds(pl.multiple_of(bit * rows, rows), rows)
    ext_part = pl.ds(pl.multiple_of(bit * near, near), near)
    grad = grad_ref[own_part, :]
    size = min(GROUP, members)
    for start in range(0, members, size):
        group = range(start, min(start + size, members))
        mixed = []
        for m in group:
            parts = [(own_ref[first_member + m, own_part, :].astype(F32) * grad).astype(BF16)]
            ext_ref, k = near_of[m]
            for s in range(sources):
                ext = ext_ref[s, k, ext_part, :].astype(F32)
                parts.append((ext * gext_ref[s, ext_part, :]).astype(BF16))
            mixed.append(jnp.concatenate(parts, axis=0))
        first = [lon_pass(x, tile) for x in mixed]
        first = [jnp.dot(lat1, x, preferred_element_type=F32).astype(BF16) for x in first]
        second = [lon_pass(x, tile) for x in first]
        second = [jnp.dot(lat2, x, preferred_element_type=F32) for x in second]
        product = own_ref[first_member + group[0], own_part, :].astype(F32) * second[0]
        for m, x in zip(group[1:], second[1:]):
            product += own_ref[first_member + m, own_part, :].astype(F32) * x
        if start > 0:
            product += out_ref[...]
        elif resume:
            product += sum_ref[...]
        if finish and start + size >= members:
            product = share * product + static_ref[own_part, :] * grad
        out_ref[...] = product


def filter_members(share, shapes, kept, first_member, total, own, ext, grad, gext, static, table):
    _, rows, lon = own.shape
    resume = total is not None
    finish = first_member + sum(e.shape[1] for e in ext) == own.shape[0]
    args = [own, grad, gext, static, table, *ext] + ([total] if resume else [])
    kernel = functools.partial(
        filter_kernel, share, shapes, kept, first_member, resume, finish
    )
    return pl.pallas_call(
        kernel,
        out_shape=jax.ShapeDtypeStruct((rows // 2, lon), F32),
        in_specs=[vmem()] * len(args),
        out_specs=vmem(),
        compiler_params=limit(14),
        name="filter_keep" if kept else "filter_send",
    )(*args)


def gather_kernel(which, field_ref, message, out_ref):
    rows, lon = field_ref.shape
    chunks = message.shape[0] // 6
    start = (lax.axis_index("member") % 2) * rows
    field = field_ref[...]
    blocks = lon // LANES
    stacked = jnp.concatenate(
        [field[:, b * LANES:(b + 1) * LANES] for b in range(blocks)], axis=0
    )
    table = jnp.concatenate(split_bf16(jnp.transpose(stacked)), axis=0)
    for n, place in enumerate(which):
        for c in range(chunks):
            at = place * chunks + c
            idx = message[at:at + 1, :].astype(jnp.int32)
            blk = (idx % lon) // LANES
            row = idx // lon - start
            inside = (row >= 0) & (row < rows)
            hot = onehot(blk, jnp.where(inside, row, -1), rows, blocks)
            found = jnp.dot(table, hot, preferred_element_type=F32)
            found = found[:LANES] + found[LANES:]
            spot = lax.broadcasted_iota(jnp.int32, found.shape, 0) == idx % LANES
            value = jnp.sum(jnp.where(spot, found, 0.0), axis=0, keepdims=True)
            out_ref[n * chunks + c:n * chunks + c + 1, :] = value


def gather_places(which, field, message):
    tail = len(which) * (message.shape[0] // 6)
    return pl.pallas_call(
        functools.partial(gather_kernel, which),
        out_shape=jax.ShapeDtypeStruct((tail, field.shape[1]), F32),
        in_specs=[vmem()] * 2,
        out_specs=vmem(),
        compiler_params=limit(8),
        name="gather_places",
    )(field, message)


def sums_kernel(second, *refs):
    tail = refs[0][...] + refs[1][...]
    message, out_ref = refs[2], refs[-1]
    chunks = message.shape[0] // 6
    part = lambda ref, k: ref[k * chunks:(k + 1) * chunks, :]
    total = lambda x: jnp.sum(jnp.sum(x, axis=0, keepdims=True), axis=1, keepdims=True)
    out_ref[...] = jnp.zeros_like(out_ref)
    reached = part(tail, 0)
    if second:
        text, totals = refs[3], refs[4:-1]
        at_place = scale_of(totals, chunks) * part(text, 0)
        coef, share = weigh(at_place, part(message, 4), part(message, 5))
        along = total(coef * (reached - at_place))
        curve = total(coef * at_place) + total(share * reached * reached)
    else:
        out_ref[:chunks, :] = part(tail, 1)
        along = total(part(message, 1) * reached)
        curve = total(part(message, 2) * reached * reached)
    out_ref[chunks:chunks + 1, :] = jnp.broadcast_to(along, (1, out_ref.shape[1]))
    out_ref[chunks + 1:chunks + 2, :] = jnp.broadcast_to(curve, (1, out_ref.shape[1]))


def sums(tails, message, text=None, totals=()):
    chunks, lon = message.shape[0] // 6, message.shape[1]
    second = text is not None
    args = [*tails, message] + ([text, *totals] if second else [])
    rows = -(-(chunks + 2) // 8) * 8
    return pl.pallas_call(
        functools.partial(sums_kernel, second),
        out_shape=jax.ShapeDtypeStruct((rows, LANES // 2 if second else lon), F32),
        in_specs=[vmem()] * len(args),
        out_specs=vmem(),
        compiler_params=limit(2),
        name="sums",
    )(*args)


def combine_kernel(chunks, count, *refs):
    pair, out_ref = refs[0], refs[-1]
    first, second = refs[1:1 + count], refs[1 + count:-1]
    scale_0 = scale_of(first, chunks)
    scale_1 = scale_of(second, chunks)
    out_ref[...] = (scale_0 * pair[0] + scale_1 * pair[1]).astype(out_ref.dtype)


def combine(pair, first, second, chunks):
    args = [pair, *first, *second]
    return pl.pallas_call(
        functools.partial(combine_kernel, chunks, len(first)),
        out_shape=jax.ShapeDtypeStruct(pair.shape[1:], BF16),
        in_specs=[vmem()] * len(args),
        out_specs=vmem(),
        compiler_params=limit(2),
        name="combine",
    )(*args)


def partner(count, bit):
    return [(j, j ^ bit) for j in range(count)]


def member_bits(count):
    bits, d = [], 1
    while d < count:
        bits.append(d)
        d *= 2
    assert d == count
    return bits


def swap(x, bit, count):
    return lax.ppermute(x, "member", partner(count, bit))


def halves(x, upper):
    half = x.shape[0] // 2
    return jnp.where(upper, x[half:], x[:half]), jnp.where(upper, x[:half], x[half:])


def reduce_with_tail(x, tail, bits, count, uppers):
    for bit in bits:
        keep, send = halves(x, uppers[bit])
        rows = keep.shape[0]
        got = swap(jnp.concatenate([send, tail], axis=0), bit, count)
        x = keep + got[:rows]
        tail = tail + got[rows:]
    return x, tail


def reduce_square(x, tail, high, low, count, uppers):
    keep, send = halves(x, uppers[high])
    near, far = halves(keep, uppers[low]), halves(send, uppers[low])
    rows = near[0].shape[0]
    total = jnp.concatenate([near[0], tail], axis=0)
    for part, bit in ((near[1], low), (far[0], high), (far[1], high | low)):
        total = total + swap(jnp.concatenate([part, tail], axis=0), bit, count)
    return total[:rows], total[rows:]


def gather_rows(x, bit, count, upper):
    other = swap(x, bit, count)
    axis = x.ndim - 2
    return jnp.concatenate([jnp.where(upper, other, x), jnp.where(upper, x, other)], axis=axis)


def join_rows(x, other, upper):
    axis = x.ndim - 2
    return jnp.concatenate([jnp.where(upper, other, x), jnp.where(upper, x, other)], axis=axis)


def gather_square(x, high, low, count, uppers):
    across, along, both = (swap(x, bit, count) for bit in (high, low, high | low))
    mine = join_rows(x, along, uppers[low])
    other = join_rows(across, both, uppers[low])
    return join_rows(mine, other, uppers[high])


def from_bands(x, count):
    if count == 2:
        return [lax.ppermute(x, "band", [(0, 1), (1, 0)])]
    up = [(i, i + 1) for i in range(count - 1)]
    down = [(j, i) for i, j in up]
    return [lax.ppermute(x, "band", up), lax.ppermute(x, "band", down)]


def band_halo(edges, count):
    if count == 2:
        return [lax.ppermute(edges[0], "band", [(0, 1), (1, 0)])]
    up = [(i, i + 1) for i in range(count - 1)]
    down = [(j, i) for i, j in up]
    return [lax.ppermute(e, "band", pairs) for e, pairs in zip(edges, (up, down))]


def local(ensemble, variance, obs_index, obs_value, obs_error, root_ranks):
    members_here, levels, lat_rows, lon = ensemble.shape
    n_member, n_band = lax.axis_size("member"), lax.axis_size("band")
    members = members_here * n_member
    chunks = obs_index.shape[1] // lon
    bits = member_bits(n_member)

    lat1, lat2 = lat_operators(levels // 2, lat_rows, n_band, HALF)
    shapes = (lat1.shape[1:], lat2.shape[1:], n_band)
    wide = max(LANES, lat1.shape[2])
    parts = [lon_tile(HALF), *lat1, *lat2]
    parts = [np.pad(p, ((0, 0), (0, wide - p.shape[1]))) for p in parts]
    table = jnp.asarray(np.concatenate(parts, axis=0), BF16)

    message, flags, *edges = prepare(
        n_band, bits, root_ranks, ensemble, obs_index, obs_value, obs_error, lon
    )
    sides = 1 if n_band == 2 else 2
    halo = band_halo(edges[:sides], n_band)
    keep, send = halves(message, flags[:1] > 0)
    message = keep + swap(send, bits[0], n_member)
    message = message + swap(message, bits[1], n_member)
    square = (bits[2], bits[3], bits[2] | bits[3])
    message = message + sum(swap(message, bit, n_member) for bit in square)
    for bit in bits[4:]:
        message = message + swap(message, bit, n_member)
    message = gather_rows(message, bits[0], n_member, flags[:1] > 0)
    around = from_bands(message, n_band)

    own = ensemble.reshape(members_here, levels * lat_rows, lon)
    near_rows = lambda part: jnp.stack(
        [h.reshape(h.shape[0], levels * REACH, lon) for h in part]
    )
    ext = [near_rows(halo)]
    uppers = {bit: flags[k:k + 1] > 0 for k, bit in enumerate(bits)}
    static = flags[-1] * variance
    static = static.reshape(levels * lat_rows, lon)
    share = ensemble_share / (members - 1)

    def direction_parts(rest, text=None, totals=(), texts=()):
        scatter = functools.partial(scatter_obs, levels, lat_rows, lon, n_band)
        grad = scatter(message, text, totals)
        gext = [
            scatter(a, texts[s] if texts else None, totals, s)
            for s, a in enumerate(around)
        ]
        filters = functools.partial(filter_members, share, shapes)
        parts = (grad, jnp.stack(gext), static, table)
        if rest:
            early = [filters(kept, 0, None, own, ext, *parts) for kept in (False, True)]
            first = ext[0].shape[1]
            late = band_halo(rest, n_band)
            late, early = lax.optimization_barrier((late, early))
            ext.append(near_rows(late))
            send = filters(False, first, early[0], own, ext[1:], *parts)
            got = swap(send, bits[0], n_member)
            field = filters(True, first, early[1], own, ext[1:], *parts) + got
        else:
            got = swap(filters(False, 0, None, own, ext, *parts), bits[0], n_member)
            field = filters(True, 0, None, own, ext, *parts) + got
        keep, send = halves(field, uppers[bits[1]])
        piece = keep + swap(send, bits[1], n_member)
        tail = gather_places((3,) if texts else (0, 3), field, message)
        tail = tail + swap(tail, bits[1], n_member)
        piece, tail = reduce_square(piece, tail, bits[2], bits[3], n_member, uppers)
        piece, tail = reduce_with_tail(piece, tail, bits[4:], n_member, uppers)
        return piece, (tail, swap(tail, bits[0], n_member))

    def band_totals(text):
        texts = from_bands(text, n_band)
        if n_band == 2:
            return [text, *texts], texts
        return [lax.psum(text, "band")], texts

    piece_0, tail = direction_parts(edges[sides:])
    text = sums(tail, message)
    totals_0, texts = band_totals(text)

    piece_1, tail = direction_parts([], text, totals_0, texts)
    totals_1, _ = band_totals(sums(tail, message, text, totals_0))
    pair = jnp.stack([piece_0, piece_1])
    for bit in bits[:3:-1]:
        pair = gather_rows(pair, bit, n_member, uppers[bit])
    pair = gather_square(pair, bits[2], bits[3], n_member, uppers)
    out = combine(pair, totals_0, totals_1, chunks)
    for bit in (bits[1], bits[0]):
        out = gather_rows(out, bit, n_member, uppers[bit])
    return out.astype(F32).reshape(levels, lat_rows, lon)


def solution(mesh):
    in_specs = (
        P("member", None, "band", None),
        P(None, "band", None),
        P("member", "band"),
        P("member", "band"),
        P("member", "band"),
        P(),
    )
    out_specs = P(None, "band", None)
    return jax.shard_map(local, mesh=mesh, in_specs=in_specs, out_specs=out_specs, check_vma=False)
```

```python
import functools

import jax
import jax.numpy as jnp
import numpy as np
from jax import lax
from jax.experimental import pallas as pl
from jax.experimental.pallas import tpu as pltpu
from jax.sharding import PartitionSpec as P


HALF = 8
REACH = 2 * HALF

huber_edge = 1.5
ensemble_share = 0.75
static_share = 0.25

LANES = 256
MIB = 1 << 20
GROUP = 8
F32 = jnp.float32
BF16 = jnp.bfloat16


def tap_matrix(distance, radius):
    offsets = np.arange(-radius, radius + 1).astype(np.float32)
    raw = np.exp(np.float32(-0.5) * (offsets / np.float32(0.5 * radius)) ** 2)
    taps = raw / np.sqrt(np.sum(raw * raw))
    entry = taps[np.clip(distance, -radius, radius) + radius]
    return np.where(np.abs(distance) <= radius, entry, 0.0).astype(np.float32)


def lon_tile(radius):
    source = np.arange(2 * LANES)[:, None] - LANES // 2
    target = np.arange(LANES)[None, :]
    return tap_matrix(source - target, radius)


def lat_block(out_level, out_row, in_level, in_row, rows_total, radius):
    entry = tap_matrix(in_row[None, :] - out_row[:, None], radius)
    inside = (out_row >= 0) & (out_row < rows_total)
    keep = (out_level[:, None] == in_level[None, :]) & inside[:, None]
    return np.where(keep, entry, 0.0)


def lat_operators(levels, rows, bands, radius):
    reach = 2 * radius
    first, second = [], []
    for band in range(bands):
        base = band * rows
        if bands == 2:
            sides = [(base + rows, base + rows) if band == 0 else (base - reach, base - radius)]
        else:
            sides = [(base - reach, base - radius), (base + rows, base + rows)]

        def row_list(start, width):
            level = np.repeat(np.arange(levels), width)
            return level, np.tile(np.arange(width), levels) + start

        own = row_list(base, rows)
        join = lambda parts: tuple(np.concatenate(p) for p in zip(*parts))
        outer = join([own] + [row_list(s[0], reach) for s in sides])
        inner = join([own] + [row_list(s[1], radius) for s in sides])
        first.append(lat_block(*inner, *outer, rows * bands, radius))
        second.append(lat_block(*own, *inner, rows * bands, radius))
    return np.stack(first), np.stack(second)


def split_bf16(x):
    hi = x.astype(BF16)
    lo = (x - hi.astype(F32)).astype(BF16)
    return hi, lo


def counter(count, width):
    column = lax.broadcasted_iota(jnp.int32, (count, LANES // 2), 0).astype(F32).astype(BF16)
    return jnp.concatenate([column] * (width // (LANES // 2)), axis=1)


def onehot(blk, row, rows, blocks):
    count = counter(rows, row.shape[1])
    one, zero = jnp.ones((), BF16), jnp.zeros((), BF16)
    parts = []
    for b in range(blocks):
        here = jnp.where(blk == b, row, -1).astype(F32).astype(BF16)
        parts.append(jnp.where(count == here, one, zero))
    return jnp.concatenate(parts, axis=0)


def limit(mebibytes):
    return pltpu.CompilerParams(vmem_limit_bytes=mebibytes * MIB)


def vmem():
    return pl.BlockSpec(memory_space=pltpu.VMEM)


def weigh(at_place, value, error):
    departure = value - at_place
    weight = huber_edge / jnp.maximum(jnp.abs(departure / error), huber_edge)
    share = weight / (error * error)
    return share * departure, share


def halo_groups(members):
    late = members // 4
    return [members - late, late] if late else [members]


def prepare_kernel(bands, bits, root_hbm, ens_hbm, idx_hbm, value_hbm, error_hbm, out_ref,
                   flag_ref, *refs):
    edges, (roots, idx_ref, value_ref, error_ref, arrived) = refs[:-5], refs[-5:]
    rows = ens_hbm.shape[2]
    chunks, lon = out_ref.shape[0] // 6, out_ref.shape[1]
    if bands == 2:
        starts = [jnp.where(lax.axis_index("band") == 0, rows - REACH, 0)]
    else:
        starts = [rows - REACH, 0]
    pairs = [(idx_hbm, idx_ref), (value_hbm, value_ref), (error_hbm, error_ref)]
    pairs.append((root_hbm, roots))
    member = 0
    for k, edge in enumerate(edges):
        side = k % len(starts)
        some = pl.ds(member, edge.shape[0])
        row = pl.ds(pl.multiple_of(starts[side], REACH), REACH)
        pairs.append((ens_hbm.at[some, :, row, :], edge))
        member += edge.shape[0] if side == len(starts) - 1 else 0
    loads = [pltpu.make_async_copy(x, y, arrived.at[k]) for k, (x, y) in enumerate(pairs)]
    for load in loads:
        load.start()
    position = lax.axis_index("member")
    for k in range(flag_ref.shape[0]):
        value = jnp.where(position == 0, static_share, 0.0)
        if k < len(bits):
            value = ((position // bits[k]) % 2).astype(F32)
        flag_ref[k:k + 1, :] = jnp.full((1, flag_ref.shape[1]), value, F32)
    for load in loads[:4]:
        load.wait()
    first, second = position == roots[0], position == roots[1]
    for c in range(chunks):
        lanes = slice(c * lon, (c + 1) * lon)
        idx = idx_ref[:, lanes].astype(F32)
        value, error = value_ref[:, lanes], error_ref[:, lanes]
        coef, share = weigh(0.0, value, error)
        for k, x in ((0, idx), (1, coef), (5, share)):
            out_ref[k * chunks + c:k * chunks + c + 1, :] = jnp.where(first, x, 0.0)
        for k, x in ((2, idx), (3, value), (4, error)):
            out_ref[k * chunks + c:k * chunks + c + 1, :] = jnp.where(second, x, 0.0)
    for load in loads[4:]:
        load.wait()


def prepare(bands, bits, roots, ensemble, index, value, error, lon):
    sides = 1 if bands == 2 else 2
    groups = halo_groups(ensemble.shape[0])
    count = sides * len(groups)
    away = pl.BlockSpec(memory_space=pl.ANY)
    assert len(bits) < 8
    inputs = [roots, ensemble, index, value, error]
    inputs = [pltpu.with_memory_space_constraint(x, pltpu.HBM) for x in inputs]
    edges = [
        jax.ShapeDtypeStruct((n, ensemble.shape[1], REACH, lon), BF16)
        for n in groups
        for _ in range(sides)
    ]
    return pl.pallas_call(
        functools.partial(prepare_kernel, bands, bits),
        out_shape=(
            jax.ShapeDtypeStruct((6 * (index.shape[1] // lon), lon), F32),
            jax.ShapeDtypeStruct((8, lon), F32),
            *edges,
        ),
        in_specs=[away] * 5,
        out_specs=[vmem()] * (2 + count),
        scratch_shapes=[
            pltpu.SMEM(roots.shape, roots.dtype),
            pltpu.VMEM(index.shape, index.dtype),
            pltpu.VMEM(index.shape, F32),
            pltpu.VMEM(index.shape, F32),
            pltpu.SemaphoreType.DMA((4 + count,)),
        ],
        compiler_params=limit(8),
        name="prepare",
    )(*inputs)


def add_onehot(idx, coef, row, acc, blocks, lanes):
    blk = (idx % (blocks * lanes)) // lanes
    lane = (idx % lanes).astype(F32).astype(BF16)
    spot = counter(lanes, idx.shape[1]) == lane
    zero = jnp.zeros((), BF16)
    side = jnp.concatenate([jnp.where(spot, x, zero) for x in split_bf16(coef)], axis=0)
    hot = onehot(blk, row, acc.shape[0] // blocks, blocks)
    acc[...] += lax.dot_general(
        hot, side, (((1,), (1,)), ((), ())), preferred_element_type=F32
    )


def total_of(totals, row):
    value = totals[0][row:row + 1, :1]
    for t in totals[1:]:
        value = value + t[row:row + 1, :1]
    return value


def scale_of(totals, chunks):
    along = total_of(totals, chunks)
    return along / (along + total_of(totals, chunks + 1))


def coefficients(second, message, chunks, text, totals, c):
    row = lambda ref, k: ref[k * chunks + c:k * chunks + c + 1, :]
    if not second:
        return row(message, 0), row(message, 1)
    at_place = scale_of(totals, chunks) * row(text, 0)
    error = row(message, 4)
    coef, _ = weigh(at_place, row(message, 3), jnp.where(error > 0, error, 1.0))
    return row(message, 2), coef


def scatter_kernel(second, rows, lon, bands, near, *refs):
    if near is not None:
        start = [rows - REACH, 0][near]
        if bands == 2:
            start = jnp.where(lax.axis_index("band") == 0, 0, rows - REACH)
    out_ref, acc = refs[-2:]
    message = refs[0]
    text, totals = (refs[1], refs[2:-2]) if second else (None, None)
    chunks = message.shape[0] // (6 if near is None else 5)
    width = out_ref.shape[0]
    acc[...] = jnp.zeros_like(acc)
    lanes = acc.shape[1] // 2
    for c in range(chunks):
        place, coef = coefficients(second, message, chunks, text, totals, c)
        idx = place.astype(jnp.int32)
        if near is None:
            row = idx // lon
        else:
            row = (idx // lon) % rows - start
            inside = (row >= 0) & (row < REACH)
            row = jnp.where(inside, (idx // (lon * rows)) * REACH + row, -1)
        add_onehot(idx, coef, row, acc, lon // lanes, lanes)
    for b in range(lon // lanes):
        part = acc[b * width:(b + 1) * width, :]
        out_ref[:, b * lanes:(b + 1) * lanes] = part[:, :lanes] + part[:, lanes:]


def scatter_obs(levels, rows, lon, bands, message, text, totals, near=None):
    second = text is not None
    width = levels * (rows if near is None else REACH)
    lanes = LANES if near is None else LANES // 2
    args = [message] + ([text, *totals] if second else [])
    return pl.pallas_call(
        functools.partial(scatter_kernel, second, rows, lon, bands, near),
        out_shape=jax.ShapeDtypeStruct((width, lon), F32),
        in_specs=[vmem()] * len(args),
        out_specs=vmem(),
        scratch_shapes=[pltpu.VMEM(((lon // lanes) * width, 2 * lanes), F32)],
        compiler_params=limit(8),
        name="scatter_own" if near is None else "scatter_near",
    )(*args)


def lon_pass(x, tile):
    rows, lon = x.shape
    half = LANES // 2
    parts = []
    for j in range(lon // LANES):
        lo, hi = j * LANES - half, (j + 1) * LANES + half
        if lo < 0:
            window = jnp.concatenate([x[:, lon + lo:], x[:, :hi]], axis=1)
        elif hi > lon:
            window = jnp.concatenate([x[:, lo:], x[:, :hi - lon]], axis=1)
        else:
            window = x[:, lo:hi]
        parts.append(window)
    stacked = jnp.concatenate(parts, axis=0)
    y = jnp.dot(stacked, tile, preferred_element_type=F32).astype(BF16)
    return jnp.concatenate([y[j * rows:(j + 1) * rows] for j in range(lon // LANES)], axis=1)


def filter_kernel(share, shapes, kept, first_member, resume, finish, *refs):
    own_ref, grad_ref, gext_ref, static_ref, table_ref = refs[:5]
    ext_refs, out_ref = refs[5:-1], refs[-1]
    sum_ref = None
    if resume:
        ext_refs, sum_ref = ext_refs[:-1], ext_refs[-1]
    bit = lax.axis_index("member") % 2
    bit = bit if kept else 1 - bit
    band = lax.axis_index("band")
    near_of = [(ref, k) for ref in ext_refs for k in range(ref.shape[1])]
    members = len(near_of)
    (rows_1, cols_1), (rows_2, cols_2), bands = shapes
    sources = ext_refs[0].shape[0]
    tile = table_ref[:2 * LANES, :LANES]
    start_1 = pl.multiple_of(2 * LANES + band * rows_1, 16)
    start_2 = pl.multiple_of(2 * LANES + bands * rows_1 + band * rows_2, 16)
    lat1 = table_ref[pl.ds(start_1, rows_1), :cols_1]
    lat2 = table_ref[pl.ds(start_2, rows_2), :cols_2]
    rows = own_ref.shape[1] // 2
    near = ext_refs[0].shape[2] // 2
    own_part = pl.ds(pl.multiple_of(bit * rows, rows), rows)
    ext_part = pl.ds(pl.multiple_of(bit * near, near), near)
    grad = grad_ref[own_part, :]
    size = min(GROUP, members)
    for start in range(0, members, size):
        group = range(start, min(start + size, members))
        mixed = []
        for m in group:
            parts = [(own_ref[first_member + m, own_part, :].astype(F32) * grad).astype(BF16)]
            ext_ref, k = near_of[m]
            for s in range(sources):
                ext = ext_ref[s, k, ext_part, :].astype(F32)
                parts.append((ext * gext_ref[s, ext_part, :]).astype(BF16))
            mixed.append(jnp.concatenate(parts, axis=0))
        first = [lon_pass(x, tile) for x in mixed]
        first = [jnp.dot(lat1, x, preferred_element_type=F32).astype(BF16) for x in first]
        second = [lon_pass(x, tile) for x in first]
        second = [jnp.dot(lat2, x, preferred_element_type=F32) for x in second]
        product = own_ref[first_member + group[0], own_part, :].astype(F32) * second[0]
        for m, x in zip(group[1:], second[1:]):
            product += own_ref[first_member + m, own_part, :].astype(F32) * x
        if start > 0:
            product += out_ref[...]
        elif resume:
            product += sum_ref[...]
        if finish and start + size >= members:
            product = share * product + static_ref[own_part, :] * grad
        out_ref[...] = product


def filter_members(share, shapes, kept, first_member, total, own, ext, grad, gext, static, table):
    _, rows, lon = own.shape
    resume = total is not None
    finish = first_member + sum(e.shape[1] for e in ext) == own.shape[0]
    args = [own, grad, gext, static, table, *ext] + ([total] if resume else [])
    kernel = functools.partial(
        filter_kernel, share, shapes, kept, first_member, resume, finish
    )
    return pl.pallas_call(
        kernel,
        out_shape=jax.ShapeDtypeStruct((rows // 2, lon), F32),
        in_specs=[vmem()] * len(args),
        out_specs=vmem(),
        compiler_params=limit(14),
        name="filter_keep" if kept else "filter_send",
    )(*args)


def gather_kernel(which, field_ref, message, out_ref):
    rows, lon = field_ref.shape
    chunks = message.shape[0] // 6
    start = (lax.axis_index("member") % 2) * rows
    field = field_ref[...]
    blocks = lon // LANES
    stacked = jnp.concatenate(
        [field[:, b * LANES:(b + 1) * LANES] for b in range(blocks)], axis=0
    )
    table = jnp.concatenate(split_bf16(jnp.transpose(stacked)), axis=0)
    for n, place in enumerate(which):
        for c in range(chunks):
            at = place * chunks + c
            idx = message[at:at + 1, :].astype(jnp.int32)
            blk = (idx % lon) // LANES
            row = idx // lon - start
            inside = (row >= 0) & (row < rows)
            hot = onehot(blk, jnp.where(inside, row, -1), rows, blocks)
            found = jnp.dot(table, hot, preferred_element_type=F32)
            found = found[:LANES] + found[LANES:]
            spot = lax.broadcasted_iota(jnp.int32, found.shape, 0) == idx % LANES
            value = jnp.sum(jnp.where(spot, found, 0.0), axis=0, keepdims=True)
            out_ref[n * chunks + c:n * chunks + c + 1, :] = value


def gather_places(which, field, message):
    tail = len(which) * (message.shape[0] // 6)
    return pl.pallas_call(
        functools.partial(gather_kernel, which),
        out_shape=jax.ShapeDtypeStruct((tail, field.shape[1]), F32),
        in_specs=[vmem()] * 2,
        out_specs=vmem(),
        compiler_params=limit(8),
        name="gather_places",
    )(field, message)


def sums_kernel(second, *refs):
    tail = refs[0][...] + refs[1][...]
    message, out_ref = refs[2], refs[-1]
    chunks = message.shape[0] // 6
    part = lambda ref, k: ref[k * chunks:(k + 1) * chunks, :]
    total = lambda x: jnp.sum(jnp.sum(x, axis=0, keepdims=True), axis=1, keepdims=True)
    out_ref[...] = jnp.zeros_like(out_ref)
    reached = part(tail, 0)
    if second:
        text, totals = refs[3], refs[4:-1]
        at_place = scale_of(totals, chunks) * part(text, 0)
        coef, share = weigh(at_place, part(message, 3), part(message, 4))
        along = total(coef * (reached - at_place))
        curve = total(coef * at_place) + total(share * reached * reached)
    else:
        out_ref[:chunks, :] = part(tail, 1)
        along = total(part(message, 1) * reached)
        curve = total(part(message, 5) * reached * reached)
    out_ref[chunks:chunks + 1, :] = jnp.broadcast_to(along, (1, out_ref.shape[1]))
    out_ref[chunks + 1:chunks + 2, :] = jnp.broadcast_to(curve, (1, out_ref.shape[1]))


def sums(tails, message, text=None, totals=()):
    chunks, lon = message.shape[0] // 6, message.shape[1]
    second = text is not None
    args = [*tails, message] + ([text, *totals] if second else [])
    rows = -(-(chunks + 2) // 8) * 8
    return pl.pallas_call(
        functools.partial(sums_kernel, second),
        out_shape=jax.ShapeDtypeStruct((rows, LANES // 2 if second else lon), F32),
        in_specs=[vmem()] * len(args),
        out_specs=vmem(),
        compiler_params=limit(2),
        name="sums",
    )(*args)


def combine_kernel(chunks, count, *refs):
    pair, out_ref = refs[0], refs[-1]
    first, second = refs[1:1 + count], refs[1 + count:-1]
    scale_0 = scale_of(first, chunks)
    scale_1 = scale_of(second, chunks)
    out_ref[...] = (scale_0 * pair[0] + scale_1 * pair[1]).astype(out_ref.dtype)


def combine(pair, first, second, chunks):
    args = [pair, *first, *second]
    return pl.pallas_call(
        functools.partial(combine_kernel, chunks, len(first)),
        out_shape=jax.ShapeDtypeStruct(pair.shape[1:], BF16),
        in_specs=[vmem()] * len(args),
        out_specs=vmem(),
        compiler_params=limit(2),
        name="combine",
    )(*args)


def partner(count, bit):
    return [(j, j ^ bit) for j in range(count)]


def member_bits(count):
    bits, d = [], 1
    while d < count:
        bits.append(d)
        d *= 2
    assert d == count
    return bits


def swap(x, bit, count):
    return lax.ppermute(x, "member", partner(count, bit))


def halves(x, upper):
    half = x.shape[0] // 2
    return jnp.where(upper, x[half:], x[:half]), jnp.where(upper, x[:half], x[half:])


def reduce_with_tail(x, tail, bits, count, uppers):
    for bit in bits:
        keep, send = halves(x, uppers[bit])
        rows = keep.shape[0]
        got = swap(jnp.concatenate([send, tail], axis=0), bit, count)
        x = keep + got[:rows]
        tail = tail + got[rows:]
    return x, tail


def reduce_square(x, tail, high, low, count, uppers):
    keep, send = halves(x, uppers[high])
    near, far = halves(keep, uppers[low]), halves(send, uppers[low])
    rows = near[0].shape[0]
    total = jnp.concatenate([near[0], tail], axis=0)
    for part, bit in zip((near[1], far[0], far[1]), (low, high, high | low)):
        total = total + swap(jnp.concatenate([part, tail], axis=0), bit, count)
    return total[:rows], total[rows:]


def gather_rows(x, bit, count, upper):
    other = swap(x, bit, count)
    axis = x.ndim - 2
    return jnp.concatenate([jnp.where(upper, other, x), jnp.where(upper, x, other)], axis=axis)


def join_rows(x, other, upper):
    axis = x.ndim - 2
    return jnp.concatenate([jnp.where(upper, other, x), jnp.where(upper, x, other)], axis=axis)


def gather_square(x, high, low, count, uppers):
    got = []
    for bit in (low, high, high | low):
        got.append(swap(x, bit, count))
    along, across, both = got
    mine = join_rows(x, along, uppers[low])
    other = join_rows(across, both, uppers[low])
    return join_rows(mine, other, uppers[high])


def from_bands(x, count):
    if count == 2:
        return [lax.ppermute(x, "band", [(0, 1), (1, 0)])]
    up = [(i, i + 1) for i in range(count - 1)]
    down = [(j, i) for i, j in up]
    return [lax.ppermute(x, "band", up), lax.ppermute(x, "band", down)]


def band_halo(edges, count):
    if count == 2:
        return [lax.ppermute(edges[0], "band", [(0, 1), (1, 0)])]
    up = [(i, i + 1) for i in range(count - 1)]
    down = [(j, i) for i, j in up]
    return [lax.ppermute(e, "band", pairs) for e, pairs in zip(edges, (up, down))]


def local(ensemble, variance, obs_index, obs_value, obs_error, root_ranks):
    members_here, levels, lat_rows, lon = ensemble.shape
    n_member, n_band = lax.axis_size("member"), lax.axis_size("band")
    members = members_here * n_member
    chunks = obs_index.shape[1] // lon
    bits = member_bits(n_member)

    lat1, lat2 = lat_operators(levels // 2, lat_rows, n_band, HALF)
    shapes = (lat1.shape[1:], lat2.shape[1:], n_band)
    wide = max(LANES, lat1.shape[2])
    parts = [lon_tile(HALF), *lat1, *lat2]
    parts = [np.pad(p, ((0, 0), (0, wide - p.shape[1]))) for p in parts]
    table = jnp.asarray(np.concatenate(parts, axis=0), BF16)

    message, flags, *edges = prepare(
        n_band, bits, root_ranks, ensemble, obs_index, obs_value, obs_error, lon
    )
    sides = 1 if n_band == 2 else 2
    halo = band_halo(edges[:sides], n_band)
    keep, send = halves(message, flags[:1] > 0)
    message = keep + swap(send, bits[0], n_member)
    message = message + swap(message, bits[1], n_member)
    square = (bits[2], bits[3], bits[2] | bits[3])
    message = message + sum(swap(message, bit, n_member) for bit in square)
    for bit in bits[4:]:
        message = message + swap(message, bit, n_member)
    message = gather_rows(message, bits[0], n_member, flags[:1] > 0)
    around = from_bands(message[:5 * chunks], n_band)

    own = ensemble.reshape(members_here, levels * lat_rows, lon)
    near_rows = lambda part: jnp.stack(
        [h.reshape(h.shape[0], levels * REACH, lon) for h in part]
    )
    ext = [near_rows(halo)]
    uppers = {bit: flags[k:k + 1] > 0 for k, bit in enumerate(bits)}
    static = flags[-1] * variance
    static = static.reshape(levels * lat_rows, lon)
    share = ensemble_share / (members - 1)

    def direction_parts(rest, text=None, totals=(), texts=()):
        scatter = functools.partial(scatter_obs, levels, lat_rows, lon, n_band)
        grad = scatter(message, text, totals)
        gext = [
            scatter(a, texts[s] if texts else None, totals, s)
            for s, a in enumerate(around)
        ]
        filters = functools.partial(filter_members, share, shapes)
        parts = (grad, jnp.stack(gext), static, table)
        if rest:
            early = [filters(kept, 0, None, own, ext, *parts) for kept in (False, True)]
            first = ext[0].shape[1]
            late = band_halo(rest, n_band)
            late, early = lax.optimization_barrier((late, early))
            ext.append(near_rows(late))
            send = filters(False, first, early[0], own, ext[1:], *parts)
            got = swap(send, bits[0], n_member)
            field = filters(True, first, early[1], own, ext[1:], *parts) + got
        else:
            got = swap(filters(False, 0, None, own, ext, *parts), bits[0], n_member)
            field = filters(True, 0, None, own, ext, *parts) + got
        keep, send = halves(field, uppers[bits[1]])
        piece = keep + swap(send, bits[1], n_member)
        tail = gather_places((2,) if texts else (0, 2), field, message)
        tail = tail + swap(tail, bits[1], n_member)
        piece, tail = reduce_square(piece, tail, bits[2], bits[3], n_member, uppers)
        piece, tail = reduce_with_tail(piece, tail, bits[4:], n_member, uppers)
        return piece, (tail, swap(tail, bits[0], n_member))

    def band_totals(text):
        texts = from_bands(text, n_band)
        if n_band == 2:
            return [text, *texts], texts
        return [lax.psum(text, "band")], texts

    piece_0, tail = direction_parts(edges[sides:])
    text = sums(tail, message)
    totals_0, texts = band_totals(text)

    piece_1, tail = direction_parts([], text, totals_0, texts)
    totals_1, _ = band_totals(sums(tail, message, text, totals_0))
    pair = jnp.stack([piece_0, piece_1])
    for bit in bits[:3:-1]:
        pair = gather_rows(pair, bit, n_member, uppers[bit])
    pair = gather_square(pair, bits[2], bits[3], n_member, uppers)
    out = combine(pair, totals_0, totals_1, chunks)
    out = gather_square(out, bits[0], bits[1], n_member, uppers)
    return out.astype(F32).reshape(levels, lat_rows, lon)


def solution(mesh):
    in_specs = (
        P("member", None, "band", None),
        P(None, "band", None),
        P("member", "band"),
        P("member", "band"),
        P("member", "band"),
        P(),
    )
    out_specs = P(None, "band", None)
    return jax.shard_map(local, mesh=mesh, in_specs=in_specs, out_specs=out_specs, check_vma=False)
```
